128 devices in a mesh: rows: 64 (over y, z, x), rhs: 2 (over core).
Axes of the slice: x: 4, y: 4, z: 4, core: 2. Of those that a mesh axis runs over, the one named last changes fastest.
Arguments:
- rhs: float32 [2, 32768, 4096], P(None, 'rows', 'rhs'), may hold values from -8 to 8
- factor: bfloat16 [2, 32768, 4, 512], P(None, 'rows', None, 'rhs'), may hold values from -0.125 to 0.125
- inverses: float32 [4, 512, 512], replicated, may hold values from -1 to 1, as said below
Outputs:
- state: float32 [2, 32768, 4096], P(None, 'rows', 'rhs')
The draws below stay inside these ranges and needn't reach their ends.
Inputs may be any that keep to these rules, and one draw needn't show every extreme that they name: Each inverses[p] is unit lower triangular: ones on the diagonal, zeros above it.
All inputs are finite; a program needn't handle non-finite values.
Results may differ from the reference program's by a relative error of at most 0.003.
Values may be sent and summed in bfloat16 or wider, within the bound.
No kernel may reach another device: no remote copies, remote signals or barrier semaphores. Data moves between devices by JAX's collectives and lax.ppermute only.
A program may use at most 128 MiB of HBM per device.

```python
import jax
import jax.numpy as jnp
from jax import lax

TILE = 512
PANELS = 4
NRHS = 4096
CYC = 2
WIDTH = 32768
N_ROWS = 64


def draw_inverses(key, part):
    values = jax.random.normal(key, (PANELS, TILE, TILE), jnp.float32)
    values = jnp.clip(values, -4.0, 4.0) * TILE ** (-0.5)
    return jnp.tril(values, -1) + jnp.eye(TILE, dtype=jnp.float32)[None]


def level_of(rng, shape, cuts, low, high):
    loudness, own = 1.0, jax.random.fold_in(rng, 6)
    for axis_at, shards_of in cuts:
        steps = jnp.exp(jax.random.uniform(jax.random.fold_in(own, axis_at), (shards_of,), jnp.float32, low / len(cuts), high / len(cuts)))
        loudness = loudness * jnp.repeat(steps, shape[axis_at] // shards_of).reshape([-1 if axis == axis_at else 1 for axis in range(len(shape))])
    return loudness


def bell_draw(key, dims, scale, reach, split=(), kind=jnp.bfloat16):
    result = jax.random.normal(key, dims, jnp.float32) * scale
    if len(split) > 0:
        result = level_of(key, dims, split, -0.22, 0.18) * result
    return jnp.clip(result, min=-reach, max=reach).astype(kind)


def setup_inputs(seed: int = 0) -> dict:
    keys = jax.random.split(jax.random.key(seed), 4)
    rhs = bell_draw(keys[0], (CYC, WIDTH, NRHS), 1.0, 8.0, ((1, 64), (2, 2)), jnp.float32)
    factor = bell_draw(keys[1], (CYC, WIDTH, PANELS, TILE), (PANELS * TILE) ** -0.5, 0.125, ((1, 64), (3, 2)))
    inverses = draw_inverses(jax.random.fold_in(keys[3], 71), 0)
    return {"rhs": rhs, "factor": factor, "inverses": inverses}


def reference(rhs, factor, inverses):
    cycles = rhs.shape[0]
    width = rhs.shape[1]
    tile_ids = jnp.arange(cycles, dtype=jnp.int32)[:, None] * N_ROWS + (jnp.arange(width, dtype=jnp.int32) // TILE)[None, :]
    state = rhs
    for panel in range(PANELS):
        pivot = state[0, panel * TILE:(panel + 1) * TILE]
        solved = jnp.dot(inverses[panel], pivot, precision=lax.Precision.HIGHEST)
        sent = lax.optimization_barrier(solved.astype(jnp.bfloat16)).astype(jnp.float32)
        state = state.at[0, panel * TILE:(panel + 1) * TILE].set(solved)
        delta = jnp.einsum("crk,kn->crn", factor[:, :, panel, :].astype(jnp.float32), sent, precision=lax.Precision.HIGHEST)
        state = state - jnp.where((tile_ids > panel)[:, :, None], delta, jnp.float32(0.0))
    return state
```

```python
import jax
import jax.numpy as jnp
from jax import lax
from jax.experimental import pallas as pl
from jax.experimental.pallas import tpu as pltpu
from jax.sharding import Mesh, PartitionSpec as P

ROWS = ("y", "z", "x")
BF = jnp.bfloat16
F32 = jnp.float32


def flat(x, y, z):
    return ((y % 4) * 4 + (z % 4)) * 4 + (x % 4)


def permute(value, moves):
    return lax.ppermute(value, ROWS, [(flat(*a), flat(*b)) for a, b in moves])


def ring(value, axis, step):
    return lax.ppermute(value, axis, [(i, (i + step) % 4) for i in range(4)])


def ring_gather(value, axis):
    at = lax.axis_index(axis)
    parts = [value] + [ring(value, axis, 4 - d) for d in (1, 2, 3)]
    both = jnp.stack(parts + parts[:3])
    return lax.dynamic_slice_in_dim(both, (4 - at) % 4, 4, 0)


def update_kernel(place_ref, factor_ref, rhs_ref, sent_ref, out_ref):
    panels = sent_ref.shape[1]
    depth = panels * sent_ref.shape[2]
    both = jnp.concatenate([sent_ref[i].reshape(depth, 128) for i in range(2)], axis=1)
    for c in range(2):
        out_ref[c] = rhs_ref[c] - jnp.dot(factor_ref[c], both, preferred_element_type=F32)
    place = place_ref[0]

    @pl.when(place < panels)
    def _():
        for i in range(2):
            out_ref[0, :, i * 128:(i + 1) * 128] = sent_ref[i, place].astype(F32)


def update(place, factor, rhs, sent):
    cycles, tile, depth = factor.shape
    cols = rhs.shape[2]
    return pl.pallas_call(
        update_kernel,
        grid=(cols // 256,),
        in_specs=[
            pl.BlockSpec(memory_space=pltpu.SMEM),
            pl.BlockSpec((cycles, tile, depth), lambda j: (0, 0, 0)),
            pl.BlockSpec((cycles, tile, 256), lambda j: (0, 0, j)),
            pl.BlockSpec((2, 4, tile, 128), lambda j: (j, 0, 0, 0)),
        ],
        out_specs=pl.BlockSpec((cycles, tile, 256), lambda j: (0, 0, j)),
        out_shape=jax.ShapeDtypeStruct(rhs.shape, F32),
        compiler_params=pltpu.CompilerParams(vmem_limit_bytes=48 << 20),
    )(place[None], factor, rhs, sent)


def local(rhs, factor, inverses):
    x, y, z = (lax.axis_index(a) for a in ("x", "y", "z"))
    core = lax.axis_index("rhs")
    place = (y * 4 + z) * 4 + x
    owner = place < 4

    tile = rhs[0]
    high = lax.reduce_precision(tile, 8, 7)
    low = (tile - high).astype(BF)
    high = high.astype(BF)
    blocks = lambda v: v.reshape(512, 16, 128).transpose(1, 0, 2)
    shards = factor[0, :, :3].reshape(16, 192, 128)
    load_a = jnp.concatenate([blocks(high), shards[:, :96]], axis=1).reshape(4, 4, 608, 128)
    load_b = jnp.concatenate([blocks(low), shards[:, 96:]], axis=1).reshape(4, 4, 608, 128)

    zero = jnp.zeros((), BF)
    hold_a = jnp.where(owner, load_a[0], zero)
    hold_b = jnp.where(owner, load_b[:, 0], zero)
    for d in (1, 3, 2):
        hold_a = hold_a + permute(load_a[d], [((i, 0, 0), (i, d, 0)) for i in range(4)])
        hold_b = hold_b + permute(load_b[:, d], [((i, 0, 0), (i, 0, d)) for i in range(4)])
    mine_a = jnp.where(z == 0, hold_a[0], zero)
    mine_b = jnp.where(y == 0, hold_b[0], zero)
    for d in (1, 3, 2):
        mine_a = mine_a + permute(hold_a[d], [((i, j, 0), (i, j, d)) for i in range(4) for j in range(4)])
        mine_b = mine_b + permute(hold_b[d], [((i, 0, j), (i, d, j)) for i in range(4) for j in range(4)])

    shard = jnp.concatenate([mine_a[512:], mine_b[512:]], axis=0)
    half = ring_gather(ring_gather(shard, "z"), "y").reshape(512, 3, 256)
    other = lax.ppermute(half, "rhs", [(0, 1), (1, 0)])
    own = jnp.where(core == 0, jnp.concatenate([half, other], axis=2), jnp.concatenate([other, half], axis=2))

    inverse = lax.dynamic_index_in_dim(inverses, x, 0, keepdims=False)
    state = mine_a[:512].astype(F32) + mine_b[:512].astype(F32)
    sent = None
    for t in range(4):
        if t > 0:
            got = sum(permute(sent, [((t - 1, j, k), (i, j, k)) for j in range(4) for k in range(4)]) for i in range(t, 4))
            state = state - jnp.dot(own[:, t - 1], got, preferred_element_type=F32)
        sent = jnp.dot(inverse, state, precision=lax.Precision.HIGHEST).astype(BF)

    everything = lax.all_gather(sent, ROWS, axis=0).reshape(16, 4, 512, 128)

    whole = lax.all_gather(factor, "rhs", axis=3, tiled=True)
    tiles = jnp.arange(2, dtype=jnp.int32) * 64 + place
    keep = tiles[:, None] > jnp.arange(4, dtype=jnp.int32)[None]
    whole = jnp.where(keep[:, None, :, None], whole, zero).reshape(2, 512, 2048)
    return update(place, whole, rhs, everything)


def solution(mesh):
    grid = Mesh(mesh.devices.reshape(4, 4, 4, 2), ("y", "z", "x", "rhs"))
    return jax.shard_map(
        local,
        mesh=grid,
        in_specs=(P(None, ROWS, "rhs"), P(None, ROWS, None, "rhs"), P()),
        out_specs=P(None, ROWS, "rhs"),
        check_vma=False,
    )
```

```python
import jax
import jax.numpy as jnp
from jax import lax
from jax.experimental import pallas as pl
from jax.experimental.pallas import tpu as pltpu
from jax.sharding import Mesh, PartitionSpec as P

ROWS = ("y", "z", "x")
BF = jnp.bfloat16
F32 = jnp.float32


def flat(x, y, z):
    return ((y % 4) * 4 + (z % 4)) * 4 + (x % 4)


def permute(value, moves):
    return lax.ppermute(value, ROWS, [(flat(*a), flat(*b)) for a, b in moves])


ODD = [(j, k) for j in range(4) for k in range(4) if (j + k) % 2 == 1]
ROUTES = [((1, 0), (2, 1)), ((0, 1), (3, 2)), ((3, 0), (2, 3)), ((0, 3), (1, 2))]


def update_kernel(place_ref, factor_ref, rhs_ref, sent_ref, out_ref):
    panels = sent_ref.shape[1]
    depth = panels * sent_ref.shape[2]
    both = jnp.concatenate([sent_ref[i].reshape(depth, 128) for i in range(2)], axis=1)
    for c in range(2):
        out_ref[c] = rhs_ref[c] - jnp.dot(factor_ref[c], both, preferred_element_type=F32)
    place = place_ref[0]

    @pl.when(place < panels)
    def _():
        for i in range(2):
            out_ref[0, :, i * 128:(i + 1) * 128] = sent_ref[i, place].astype(F32)


def update(place, factor, rhs, sent):
    cycles, tile, depth = factor.shape
    cols = rhs.shape[2]
    return pl.pallas_call(
        update_kernel,
        grid=(cols // 256,),
        in_specs=[
            pl.BlockSpec(memory_space=pltpu.SMEM),
            pl.BlockSpec((cycles, tile, depth), lambda j: (0, 0, 0)),
            pl.BlockSpec((cycles, tile, 256), lambda j: (0, 0, j)),
            pl.BlockSpec((2, 4, tile, 128), lambda j: (j, 0, 0, 0)),
        ],
        out_specs=pl.BlockSpec((cycles, tile, 256), lambda j: (0, 0, j)),
        out_shape=jax.ShapeDtypeStruct(rhs.shape, F32),
        compiler_params=pltpu.CompilerParams(vmem_limit_bytes=48 << 20),
    )(place[None], factor, rhs, sent)


def local(rhs, factor, inverses):
    x, y, z = (lax.axis_index(a) for a in ("x", "y", "z"))
    core = lax.axis_index("rhs")
    place = (y * 4 + z) * 4 + x
    owner = place < 4

    mask = jnp.where(owner, factor[0, :, :3], jnp.zeros((), BF)).transpose(1, 0, 2)
    half = lax.psum(mask, ("y", "z"))
    other = lax.ppermute(half, "rhs", [(0, 1), (1, 0)])
    own = jnp.where(core == 0, jnp.concatenate([half, other], axis=2), jnp.concatenate([other, half], axis=2))

    def piece(site):
        at = (site[0] * 2 + site[1] // 2) * 256
        return rhs[0, :, at:at + 256]

    def from_owner(value, site):
        return permute(value, [((i, 0, 0), (i,) + site) for i in range(4)])

    hold = sum(from_owner(piece(far), near) for near, far in ROUTES)
    state = sum(from_owner(piece(near), near) for near, far in ROUTES)
    state = state + permute(hold, [((i,) + near, (i,) + far) for near, far in ROUTES for i in range(4)])

    inverse = lax.dynamic_index_in_dim(inverses, x, 0, keepdims=False)
    sent = None
    for t in range(4):
        if t > 0:
            got = sum(permute(sent, [((t - 1, j, k), (i, j, k)) for j, k in ODD]) for i in range(t, 4))
            state = state - jnp.dot(own[t - 1], got, preferred_element_type=F32)
        sent = jnp.dot(inverse, state, precision=lax.Precision.HIGHEST).astype(BF)

    left, right = sent[:, :128], sent[:, 128:]
    even = z % 2 == 0
    give = permute(jnp.where(even, right, left), [((i, j, k), (i, j, k ^ 1)) for j, k in ODD for i in range(4)])
    share = jnp.where((y + z) % 2 == 1, jnp.where(even, left, right), give)
    everything = lax.all_gather(share, ROWS, axis=0).reshape(16, 4, 512, 128)

    zero = jnp.zeros((), BF)
    whole = lax.all_gather(factor, "rhs", axis=3, tiled=True)
    tiles = jnp.arange(2, dtype=jnp.int32) * 64 + place
    keep = tiles[:, None] > jnp.arange(4, dtype=jnp.int32)[None]
    whole = jnp.where(keep[:, None, :, None], whole, zero).reshape(2, 512, 2048)
    return update(place, whole, rhs, everything)


def solution(mesh):
    grid = Mesh(mesh.devices.reshape(4, 4, 4, 2), ("y", "z", "x", "rhs"))
    return jax.shard_map(
        local,
        mesh=grid,
        in_specs=(P(None, ROWS, "rhs"), P(None, ROWS, None, "rhs"), P()),
        out_specs=P(None, ROWS, "rhs"),
        check_vma=False,
    )
```

```python
import jax
import jax.numpy as jnp
from jax import lax
from jax.experimental import pallas as pl
from jax.experimental.pallas import tpu as pltpu
from jax.sharding import Mesh, PartitionSpec as P

ROWS = ("y", "z", "x")
BF = jnp.bfloat16
F32 = jnp.float32


def flat(x, y, z):
    return ((y % 4) * 4 + (z % 4)) * 4 + (x % 4)


def permute(value, moves):
    return lax.ppermute(value, ROWS, [(flat(*a), flat(*b)) for a, b in moves])


ODD = [(j, k) for j in range(4) for k in range(4) if (j + k) % 2 == 1]
ROUTES = [((1, 0), (2, 1)), ((0, 1), (3, 2)), ((3, 0), (2, 3)), ((0, 3), (1, 2))]


def update_kernel(place_ref, factor_ref, rhs_ref, sent_ref, out_ref):
    panels = sent_ref.shape[1]
    depth = panels * sent_ref.shape[2]
    both = jnp.concatenate([sent_ref[i].reshape(depth, 128) for i in range(2)], axis=1)
    for c in range(2):
        out_ref[c] = rhs_ref[c] - jnp.dot(factor_ref[c], both, preferred_element_type=F32)
    place = place_ref[0]

    @pl.when(place < panels)
    def _():
        for i in range(2):
            out_ref[0, :, i * 128:(i + 1) * 128] = sent_ref[i, place].astype(F32)


def update(place, factor, rhs, sent):
    cycles, tile, depth = factor.shape
    cols = rhs.shape[2]
    return pl.pallas_call(
        update_kernel,
        grid=(cols // 256,),
        in_specs=[
            pl.BlockSpec(memory_space=pltpu.SMEM),
            pl.BlockSpec((cycles, tile, depth), lambda j: (0, 0, 0)),
            pl.BlockSpec((cycles, tile, 256), lambda j: (0, 0, j)),
            pl.BlockSpec((2, 4, tile, 128), lambda j: (j, 0, 0, 0)),
        ],
        out_specs=pl.BlockSpec((cycles, tile, 256), lambda j: (0, 0, j)),
        out_shape=jax.ShapeDtypeStruct(rhs.shape, F32),
        compiler_params=pltpu.CompilerParams(vmem_limit_bytes=48 << 20),
    )(place[None], factor, rhs, sent)


def local(rhs, factor, inverses):
    x, y, z = (lax.axis_index(a) for a in ("x", "y", "z"))
    core = lax.axis_index("rhs")
    place = (y * 4 + z) * 4 + x
    owner = place < 4

    def piece(site):
        at = (site[0] * 2 + site[1] // 2) * 256
        return rhs[0, :, at:at + 256]

    def from_owner(value, site, planes=(0, 1, 2, 3)):
        return permute(value, [((i, 0, 0), (i,) + site) for i in planes])

    def to_far(value, planes=(0, 1, 2, 3)):
        return permute(value, [((i,) + near, (i,) + far) for near, far in ROUTES for i in planes])

    def hop(value, start, end):
        return permute(value, [((start, j, k), (end, j, k)) for j, k in ODD])

    hold = sum(from_owner(piece(far), near) for near, far in ROUTES)
    state = sum(from_owner(piece(near), near) for near, far in ROUTES)
    first, state = lax.optimization_barrier((factor[0, :, 0], state))
    state = state + to_far(hold)
    rest = factor[0, :, 1:3].transpose(1, 0, 2)

    def spread(value, planes):
        near = sum(from_owner(value, site, planes) for site, _ in ROUTES)
        mine = near + to_far(near, planes)
        return mine, lax.ppermute(mine, "rhs", [(0, 1), (1, 0)])

    first = spread(first, (1, 2, 3))
    rest, _ = lax.optimization_barrier((rest, first[0]))
    rest = spread(rest, (2, 3))
    blocks = [first, [v[0] for v in rest], [v[1] for v in rest]]

    def reduce(state, block, got):
        mine = lax.dynamic_slice_in_dim(got, core * 256, 256, 0)
        other = lax.dynamic_slice_in_dim(got, 256 - core * 256, 256, 0)
        dot = lambda a, b: jnp.dot(a, b, preferred_element_type=F32)
        return state - dot(block[0], mine) - dot(block[1], other)

    inverse = lax.dynamic_index_in_dim(inverses, x, 0, keepdims=False)
    solve = lambda s: jnp.dot(inverse, s, precision=lax.Precision.HIGHEST).astype(BF)
    sent = solve(state)
    at_1 = hop(sent, 0, 1)
    at_3 = hop(sent, 0, 3)
    at_2 = hop(at_3, 3, 2)
    state = reduce(state, blocks[0], at_1 + at_3 + at_2)
    sent = solve(state)
    at_2 = hop(sent, 1, 2)
    at_0 = hop(sent, 1, 0)
    at_3 = hop(at_0, 0, 3)
    state = reduce(state, blocks[1], at_2 + at_3)
    sent = solve(state)
    state = reduce(state, blocks[2], hop(sent, 2, 3))
    sent = solve(state)

    left, right = sent[:, :128], sent[:, 128:]
    even = z % 2 == 0
    give = permute(jnp.where(even, right, left), [((i, j, k), (i, j, k ^ 1)) for j, k in ODD for i in range(4)])
    share = jnp.where((y + z) % 2 == 1, jnp.where(even, left, right), give)
    everything = lax.all_gather(share, ROWS, axis=0).reshape(16, 4, 512, 128)

    zero = jnp.zeros((), BF)
    whole = lax.all_gather(factor, "rhs", axis=3, tiled=True)
    tiles = jnp.arange(2, dtype=jnp.int32) * 64 + place
    keep = tiles[:, None] > jnp.arange(4, dtype=jnp.int32)[None]
    whole = jnp.where(keep[:, None, :, None], whole, zero).reshape(2, 512, 2048)
    return update(place, whole, rhs, everything)


def solution(mesh):
    grid = Mesh(mesh.devices.reshape(4, 4, 4, 2), ("y", "z", "x", "rhs"))
    return jax.shard_map(
        local,
        mesh=grid,
        in_specs=(P(None, ROWS, "rhs"), P(None, ROWS, None, "rhs"), P()),
        out_specs=P(None, ROWS, "rhs"),
        check_vma=False,
    )
```

```python
import jax
import jax.numpy as jnp
from jax import lax
from jax.experimental import pallas as pl
from jax.experimental.pallas import tpu as pltpu
from jax.sharding import Mesh, PartitionSpec as P

ROWS = ("y", "z", "x")
BF = jnp.bfloat16
F32 = jnp.float32
ALL = [(j, k) for j in range(4) for k in range(4)]
ORDERS = (
    (("y", 1), ("y", 3), ("z", 1), ("z", 3)),
    (("y", 3), ("y", 1), ("z", 3), ("z", 1)),
    (("z", 1), ("z", 3), ("y", 1), ("y", 3)),
    (("z", 3), ("z", 1), ("y", 3), ("y", 1)),
)


def flat(x, y, z):
    return ((y % 4) * 4 + (z % 4)) * 4 + (x % 4)


def permute(value, moves):
    return lax.ppermute(value, ROWS, [(flat(*a), flat(*b)) for a, b in moves])


def hop(value, *planes):
    return permute(value, [((a, j, k), (b, j, k)) for a, b in planes for j, k in ALL])


def ring(value, axis, step):
    return lax.ppermute(value, axis, [(i, (i + step) % 4) for i in range(4)])


def ring_gather(value, axis):
    at = lax.axis_index(axis)
    parts = [value] + [ring(value, axis, 4 - d) for d in (1, 2, 3)]
    both = jnp.stack(parts + parts[:3])
    return lax.dynamic_slice_in_dim(both, (4 - at) % 4, 4, 0)


def swap(value, axis, flip):
    return lax.ppermute(value, axis, [(i, i ^ flip) for i in range(4)])


def spread(parts):
    parts = [p[None] for p in parts]
    for step in range(4):
        got = [swap(p, *order[step]) for p, order in zip(parts, ORDERS)]
        parts = [jnp.concatenate([p, g], axis=0) for p, g in zip(parts, got)]
    return parts


def places(y, z):
    sites = jnp.arange(16, dtype=jnp.int32)
    tables = []
    for order in ORDERS:
        off = {"y": (sites // 4) ^ y, "z": (sites % 4) ^ z}
        total = jnp.zeros_like(sites)
        for step, (axis, flip) in enumerate(order):
            o = off[axis]
            upper = o >> 1
            bit = upper if flip == 3 else (o & 1) ^ upper
            total = total + (bit << step)
        tables.append(total)
    return jnp.stack(tables).reshape(-1)


def update_kernel(scalars, factor_ref, rhs_ref, early_ref, *rest):
    late, out_ref, sent_ref = rest[:8], rest[8], rest[9]
    for h in range(2):
        lanes = slice(h * 128, (h + 1) * 128)
        sent_ref[:1024, lanes] = early_ref[h]
        for p in range(4):
            sent_ref[1024 + p * 256:1280 + p * 256, lanes] = late[p * 2 + h][0]
    for c in range(2):
        out_ref[c] = rhs_ref[c] - jnp.dot(factor_ref[c], sent_ref[...], preferred_element_type=F32)
    place = scalars[64]

    @pl.when(place < 4)
    def _():
        out_ref[0] = sent_ref[pl.ds(pl.multiple_of(place * 512, 512), 512), :].astype(F32)


def update(scalars, factor, rhs, early, late):
    cycles, tile, depth = factor.shape
    late_specs = [
        pl.BlockSpec((1, 256, 128), lambda j, s, p=p, h=h: (s[p * 16 + 2 * j + h], 0, 0))
        for p in range(4) for h in range(2)
    ]
    return pl.pallas_call(
        update_kernel,
        grid_spec=pltpu.PrefetchScalarGridSpec(
            num_scalar_prefetch=1,
            grid=(rhs.shape[2] // 256,),
            in_specs=[
                pl.BlockSpec((cycles, tile, depth), lambda j, s: (0, 0, 0)),
                pl.BlockSpec((cycles, tile, 256), lambda j, s: (0, 0, j)),
                pl.BlockSpec((2, 1024, 128), lambda j, s: (j, 0, 0)),
            ] + late_specs,
            out_specs=pl.BlockSpec((cycles, tile, 256), lambda j, s: (0, 0, j)),
            scratch_shapes=[pltpu.VMEM((depth, 256), BF)],
        ),
        out_shape=jax.ShapeDtypeStruct(rhs.shape, F32),
        compiler_params=pltpu.CompilerParams(vmem_limit_bytes=48 << 20),
    )(scalars, factor, rhs, early, *[late[p] for p in range(4) for _ in range(2)])


def local(rhs, factor, inverses):
    x, y, z = (lax.axis_index(a) for a in ("x", "y", "z"))
    core = lax.axis_index("rhs")
    place = (y * 4 + z) * 4 + x
    owner = place < 4
    zero = jnp.zeros((), BF)

    def high(slab):
        return lax.reduce_precision(slab, 8, 7).astype(BF)

    def low(slab):
        return (slab - lax.reduce_precision(slab, 8, 7)).astype(BF)

    shards = factor[0, :, :3].reshape(768, 512)

    def load_a(d):
        return jnp.concatenate([high(rhs[0, :, d * 512:(d + 1) * 512]), shards[d * 96:(d + 1) * 96]], axis=0)

    def load_b(d):
        slab = jnp.concatenate([rhs[0, :, j * 512 + d * 128:j * 512 + (d + 1) * 128] for j in range(4)], axis=1)
        return jnp.concatenate([low(slab), shards[384 + d * 96:384 + (d + 1) * 96]], axis=0)

    hold_a = jnp.where(owner, load_a(0), zero)
    hold_b = jnp.where(owner, load_b(0), zero)
    for d in (1, 3, 2):
        hold_a = hold_a + permute(load_a(d), [((i, 0, 0), (i, d, 0)) for i in range(4)])
        hold_b = hold_b + permute(load_b(d), [((i, 0, 0), (i, 0, d)) for i in range(4)])
    mine_a = jnp.where(z == 0, hold_a[:, :128], zero)
    mine_b = jnp.where(y == 0, hold_b[:, :128], zero)
    for d in (1, 3, 2):
        cut = slice(d * 128, (d + 1) * 128)
        mine_a = mine_a + permute(hold_a[:, cut], [((i, j, 0), (i, j, d)) for i in range(4) for j in range(4)])
        mine_b = mine_b + permute(hold_b[:, cut], [((i, 0, j), (i, d, j)) for i in range(4) for j in range(4)])

    shard = jnp.concatenate([mine_a[512:], mine_b[512:]], axis=0)
    every = ring_gather(ring_gather(shard, "z"), "y")
    top = every[:, :, :96].transpose(0, 2, 1, 3).reshape(384, 512)
    low_part = every[:, :, 96:].transpose(1, 2, 0, 3).reshape(384, 512)
    half = jnp.concatenate([top, low_part], axis=0).reshape(512, 3, 256).transpose(1, 0, 2)
    other = lax.ppermute(half, "rhs", [(0, 1), (1, 0)])

    def reduce(state, panel, got):
        mine = lax.dynamic_slice_in_dim(got, core * 256, 256, 0)
        rest = lax.dynamic_slice_in_dim(got, 256 - core * 256, 256, 0)
        dot = lambda a, b: jnp.dot(a, b, preferred_element_type=F32)
        return state - dot(half[panel], mine) - dot(other[panel], rest)

    inverse = lax.dynamic_index_in_dim(inverses, x, 0, keepdims=False)
    solve = lambda s: jnp.dot(inverse, s, precision=lax.Precision.HIGHEST).astype(BF)
    state = mine_a[:512].astype(F32) + mine_b[:512].astype(F32)

    sent = solve(state)
    got = hop(sent, (0, 1)) + hop(sent, (0, 3)) + hop(sent, (0, 2))
    panel_0 = jnp.where(x == 0, sent, got)
    state = reduce(state, 0, got)
    sent = solve(state)
    got = hop(sent, (1, 2)) + hop(sent, (1, 3))
    panel_1 = jnp.where(x == 1, sent, got + hop(sent, (1, 0)))
    early = lax.all_gather(jnp.concatenate([panel_0, panel_1], axis=0), ("y", "z"), axis=0)
    state = reduce(state, 1, got)
    sent = solve(state)
    got = hop(sent, (2, 3))
    state = reduce(state, 2, got)
    sent = solve(state)
    back = hop(sent, (2, 1), (3, 2))
    far = hop(sent, (2, 0), (3, 1))
    wrap = hop(sent, (3, 0))
    panel_2 = jnp.where(x == 2, sent, jnp.where(x == 3, got, jnp.where(x == 1, back, far)))
    panel_3 = jnp.where(x == 3, sent, jnp.where(x == 2, back, jnp.where(x == 1, far, wrap)))
    late = spread([panel_2[:256], panel_2[256:], panel_3[:256], panel_3[256:]])

    whole = lax.all_gather(factor, "rhs", axis=3, tiled=True)
    tiles = jnp.arange(2, dtype=jnp.int32) * 64 + place
    keep = tiles[:, None] > jnp.arange(4, dtype=jnp.int32)[None]
    whole = jnp.where(keep[:, None, :, None], whole, zero).reshape(2, 512, 2048)
    scalars = jnp.concatenate([places(y, z), place[None]]).astype(jnp.int32)
    return update(scalars, whole, rhs, early, late)


def solution(mesh):
    grid = Mesh(mesh.devices.reshape(4, 4, 4, 2), ("y", "z", "x", "rhs"))
    return jax.shard_map(
        local,
        mesh=grid,
        in_specs=(P(None, ROWS, "rhs"), P(None, ROWS, None, "rhs"), P()),
        out_specs=P(None, ROWS, "rhs"),
        check_vma=False,
    )
```

```python
import jax
import jax.numpy as jnp
from jax import lax
from jax.experimental import pallas as pl
from jax.experimental.pallas import tpu as pltpu
from jax.sharding import Mesh, PartitionSpec as P

ROWS = ("y", "z", "x")
BF = jnp.bfloat16
F32 = jnp.float32
ALL = [(j, k) for j in range(4) for k in range(4)]
ORDERS = (
    (("y", 1), ("y", 3), ("z", 1), ("z", 3)),
    (("y", 3), ("y", 1), ("z", 3), ("z", 1)),
    (("z", 1), ("z", 3), ("y", 1), ("y", 3)),
    (("z", 3), ("z", 1), ("y", 3), ("y", 1)),
)


def flat(x, y, z):
    return ((y % 4) * 4 + (z % 4)) * 4 + (x % 4)


def permute(value, moves):
    return lax.ppermute(value, ROWS, [(flat(*a), flat(*b)) for a, b in moves])


def hop(value, *planes):
    return permute(value, [((a, j, k), (b, j, k)) for a, b in planes for j, k in ALL])


def ring(value, axis, step):
    return lax.ppermute(value, axis, [(i, (i + step) % 4) for i in range(4)])


def ring_gather(value, axis):
    at = lax.axis_index(axis)
    parts = [value] + [ring(value, axis, 4 - d) for d in (1, 2, 3)]
    both = jnp.stack(parts + parts[:3])
    return lax.dynamic_slice_in_dim(both, (4 - at) % 4, 4, 0)


def swap(value, axis, flip):
    return lax.ppermute(value, axis, [(i, i ^ flip) for i in range(4)])


def spread(parts, whole):
    parts = [p[None] for p in parts]
    for step in range(4):
        got = [swap(p, *order[step]) for p, order in zip(parts, ORDERS)]
        if step == 3:
            whole, *got = lax.optimization_barrier((whole, *got))
        parts = [jnp.concatenate([p, g], axis=0) for p, g in zip(parts, got)]
    return parts, whole


def places(y, z):
    sites = jnp.arange(16, dtype=jnp.int32)
    tables = []
    for order in ORDERS:
        off = {"y": (sites // 4) ^ y, "z": (sites % 4) ^ z}
        total = jnp.zeros_like(sites)
        for step, (axis, flip) in enumerate(order):
            o = off[axis]
            upper = o >> 1
            bit = upper if flip == 3 else (o & 1) ^ upper
            total = total + (bit << step)
        tables.append(total)
    return jnp.stack(tables).reshape(-1)


def split(value):
    high = value.astype(BF)
    return high, (value - high.astype(F32)).astype(BF)


def put_piece(factor_ref, base, out_ref):
    for u in range(12):
        rows = slice(base + u % 2 * 32, base + u % 2 * 32 + 32)
        at = 512 + u % 3 * 32
        out_ref[at:at + 32, u // 3 * 128:(u // 3 + 1) * 128] = factor_ref[rows, u // 2 * 128:(u // 2 + 1) * 128]


def load_a_kernel(rhs_ref, factor_ref, *outs):
    for d in range(4):
        outs[d][:512] = rhs_ref[0, :, d * 512:(d + 1) * 512].astype(BF)
        put_piece(factor_ref, d * 64, outs[d])


def load_b_kernel(rhs_ref, factor_ref, *outs):
    for d in range(4):
        for j in range(4):
            at = j * 512 + d * 128
            outs[d][:512, j * 128:(j + 1) * 128] = split(rhs_ref[0, :, at:at + 128])[1]
        put_piece(factor_ref, 256 + d * 64, outs[d])


def loads(kernel, rhs, factor):
    return pl.pallas_call(
        kernel,
        grid=(1,),
        in_specs=[pl.BlockSpec((1, 512, 2048), lambda i: (0, 0, 0)), pl.BlockSpec((512, 1024), lambda i: (0, 0))],
        out_specs=[pl.BlockSpec((608, 512), lambda i: (0, 0))] * 4,
        out_shape=[jax.ShapeDtypeStruct((608, 512), BF)] * 4,
        compiler_params=pltpu.CompilerParams(vmem_limit_bytes=40 << 20),
    )(rhs, factor)


def step_kernel(first, scalars, state_ref, high_ref, low_ref, *refs):
    dot = lambda a, b: jnp.dot(a, b, preferred_element_type=F32)
    state = state_ref[...]
    if first:
        sent_ref, = refs
    else:
        mine_ref, other_ref, got_ref, next_ref, sent_ref = refs
        swap = scalars[0] == 1
        left = jnp.where(swap, other_ref[0], mine_ref[0])
        right = jnp.where(swap, mine_ref[0], other_ref[0])
        state = state - dot(left, got_ref[:256]) - dot(right, got_ref[256:])
        next_ref[...] = state
    high, low = split(state)
    sent_ref[...] = (dot(high_ref[...], high) + dot(high_ref[...], low) + dot(low_ref[...], high)).astype(BF)


def step(core, state, inverse, mine=None, other=None, panel=0, got=None):
    first = got is None
    full = lambda shape: pl.BlockSpec(shape, lambda i, s: (0, 0))
    part = pl.BlockSpec((1, 512, 256), lambda i, s: (panel, 0, 0))
    tall, square = full((512, 128)), full((512, 512))
    sent = jax.ShapeDtypeStruct((512, 128), BF)
    new = jax.ShapeDtypeStruct((512, 128), F32)
    return pl.pallas_call(
        lambda *refs: step_kernel(first, *refs),
        grid_spec=pltpu.PrefetchScalarGridSpec(
            num_scalar_prefetch=1,
            grid=(1,),
            in_specs=[tall, square, square] + ([] if first else [part, part, tall]),
            out_specs=tall if first else [tall, tall],
        ),
        out_shape=sent if first else [new, sent],
        compiler_params=pltpu.CompilerParams(vmem_limit_bytes=32 << 20),
    )(core[None], state, *inverse, *([] if first else [mine, other, got]))


def update_kernel(scalars, factor_ref, rhs_ref, early_ref, *rest):
    late, out_ref, sent_ref = rest[:8], rest[8], rest[9]
    for h in range(2):
        lanes = slice(h * 128, (h + 1) * 128)
        sent_ref[:1024, lanes] = early_ref[h]
        for p in range(4):
            sent_ref[1024 + p * 256:1280 + p * 256, lanes] = late[p * 2 + h][0]
    for c in range(2):
        out_ref[c] = rhs_ref[c] - jnp.dot(factor_ref[c], sent_ref[...], preferred_element_type=F32)
    place = scalars[64]

    @pl.when(place < 4)
    def _():
        out_ref[0] = sent_ref[pl.ds(pl.multiple_of(place * 512, 512), 512), :].astype(F32)


def update(scalars, factor, rhs, early, late):
    cycles, tile, depth = factor.shape
    late_specs = [
        pl.BlockSpec((1, 256, 128), lambda j, s, p=p, h=h: (s[p * 16 + 2 * j + h], 0, 0))
        for p in range(4) for h in range(2)
    ]
    return pl.pallas_call(
        update_kernel,
        grid_spec=pltpu.PrefetchScalarGridSpec(
            num_scalar_prefetch=1,
            grid=(rhs.shape[2] // 256,),
            in_specs=[
                pl.BlockSpec((cycles, tile, depth), lambda j, s: (0, 0, 0)),
                pl.BlockSpec((cycles, tile, 256), lambda j, s: (0, 0, j)),
                pl.BlockSpec((2, 1024, 128), lambda j, s: (j, 0, 0)),
            ] + late_specs,
            out_specs=pl.BlockSpec((cycles, tile, 256), lambda j, s: (0, 0, j)),
            scratch_shapes=[pltpu.VMEM((depth, 256), BF)],
        ),
        out_shape=jax.ShapeDtypeStruct(rhs.shape, F32),
        compiler_params=pltpu.CompilerParams(vmem_limit_bytes=48 << 20),
    )(scalars, factor, rhs, early, *[late[p] for p in range(4) for _ in range(2)])


def local(rhs, factor, inverses):
    x, y, z = (lax.axis_index(a) for a in ("x", "y", "z"))
    core = lax.axis_index("rhs")
    place = (y * 4 + z) * 4 + x
    owner = place < 4
    zero = jnp.zeros((), BF)

    tile = factor[0].reshape(512, 1024)
    load_a = loads(load_a_kernel, rhs, tile)
    load_b = loads(load_b_kernel, rhs, tile)

    def stage(bundles, axis):
        hold = jnp.where(owner, bundles[0], zero)
        for d in (1, 3, 2):
            end = lambda i: (i, d, 0) if axis == "y" else (i, 0, d)
            hold = hold + permute(bundles[d], [((i, 0, 0), end(i)) for i in range(4)])
        return hold

    def finish(hold, axis):
        tail = [hold[512:, k * 128:(k + 1) * 128] for k in range(4)]
        message = lambda d: jnp.concatenate([hold[:512, d * 128:(d + 1) * 128]] + tail, axis=0)
        mine = jnp.where((z if axis == "y" else y) == 0, message(0), zero)
        for d in (1, 3, 2):
            if axis == "y":
                moves = [((i, j, 0), (i, j, d)) for i in range(4) for j in range(4)]
            else:
                moves = [((i, 0, j), (i, d, j)) for i in range(4) for j in range(4)]
            mine = mine + permute(message(d), moves)
        return mine

    whole = lax.all_gather(factor, "rhs", axis=3, tiled=True)
    tiles = jnp.arange(2, dtype=jnp.int32) * 64 + place
    keep = tiles[:, None] > jnp.arange(4, dtype=jnp.int32)[None]
    whole = jnp.where(keep[:, None, :, None], whole, zero).reshape(2, 512, 2048)

    hold_a = stage(load_a, "y")
    hold_b = stage(load_b, "z")
    mine_a = finish(hold_a, "y")
    mine_b = finish(hold_b, "z")

    top = ring_gather(mine_a[512:], "y")
    bottom = ring_gather(mine_b[512:], "z")
    half = jnp.concatenate([top, bottom], axis=0).reshape(8, 3, 2, 64, 128).transpose(1, 0, 3, 2, 4).reshape(3, 512, 256)
    other = lax.ppermute(half, "rhs", [(0, 1), (1, 0)])

    inverse = lax.dynamic_index_in_dim(inverses, x, 0, keepdims=False)
    rounded = lax.reduce_precision(inverse, 8, 7)
    inverse = (rounded.astype(BF), (inverse - rounded).astype(BF))
    core = core.astype(jnp.int32)
    state = mine_a[:512].astype(F32) + mine_b[:512].astype(F32)
    state, *inverse = lax.optimization_barrier((state, *inverse))
    advance = lambda state, panel, got: step(core, state, inverse, half, other, panel, got)

    sent = step(core, state, inverse)
    got = hop(sent, (0, 1)) + hop(sent, (0, 3)) + hop(sent, (0, 2))
    panel_0 = jnp.where(x == 0, sent, got)
    state, sent = advance(state, 0, got)
    got = hop(sent, (1, 2)) + hop(sent, (1, 3))
    panel_1 = jnp.where(x == 1, sent, got + hop(sent, (1, 0)))
    early = lax.all_gather(jnp.concatenate([panel_0, panel_1], axis=0), ("y", "z"), axis=0)
    state, sent = advance(state, 1, got)
    got = hop(sent, (2, 3))
    state, sent = advance(state, 2, got)
    back = hop(sent, (2, 1), (3, 2))
    far = hop(sent, (2, 0), (3, 1))
    wrap = hop(sent, (3, 0))
    panel_2 = jnp.where(x == 2, sent, jnp.where(x == 3, got, jnp.where(x == 1, back, far)))
    panel_3 = jnp.where(x == 3, sent, jnp.where(x == 2, back, jnp.where(x == 1, far, wrap)))
    late, whole = spread([panel_2[:256], panel_2[256:], panel_3[:256], panel_3[256:]], whole)

    scalars = jnp.concatenate([places(y, z), place[None]]).astype(jnp.int32)
    return update(scalars, whole, rhs, early, late)


def solution(mesh):
    grid = Mesh(mesh.devices.reshape(4, 4, 4, 2), ("y", "z", "x", "rhs"))
    return jax.shard_map(
        local,
        mesh=grid,
        in_specs=(P(None, ROWS, "rhs"), P(None, ROWS, None, "rhs"), P()),
        out_specs=P(None, ROWS, "rhs"),
        check_vma=False,
    )
```

```python
import jax
import jax.numpy as jnp
from jax import lax
from jax.experimental import pallas as pl
from jax.experimental.pallas import tpu as pltpu
from jax.sharding import Mesh, PartitionSpec as P

ROWS = ("y", "z", "x")
BF = jnp.bfloat16
F32 = jnp.float32
ALL = [(j, k) for j in range(4) for k in range(4)]
ORDERS = (
    (("y", 1), ("y", 3), ("z", 1), ("z", 3)),
    (("y", 3), ("y", 1), ("z", 3), ("z", 1)),
    (("z", 1), ("z", 3), ("y", 1), ("y", 3)),
    (("z", 3), ("z", 1), ("y", 3), ("y", 1)),
)


def flat(x, y, z):
    return ((y % 4) * 4 + (z % 4)) * 4 + (x % 4)


def permute(value, moves):
    return lax.ppermute(value, ROWS, [(flat(*a), flat(*b)) for a, b in moves])


def hop(value, *planes):
    return permute(value, [((a, j, k), (b, j, k)) for a, b in planes for j, k in ALL])


def ring(value, axis, step):
    return lax.ppermute(value, axis, [(i, (i + step) % 4) for i in range(4)])


def ring_gather(value, axis):
    at = lax.axis_index(axis)
    parts = [value] + [ring(value, axis, 4 - d) for d in (1, 2, 3)]
    both = jnp.stack(parts + parts[:3])
    return lax.dynamic_slice_in_dim(both, (4 - at) % 4, 4, 0)


def swap(value, axis, flip):
    return lax.ppermute(value, axis, [(i, i ^ flip) for i in range(4)])


def spread(parts, whole):
    parts = [p[None] for p in parts]
    for step in range(3):
        got = [swap(p, *order[step]) for p, order in zip(parts, ORDERS)]
        parts = [jnp.concatenate([p, g], axis=0) for p, g in zip(parts, got)]
    got = [swap(p, *order[3]) for p, order in zip(parts, ORDERS)]
    whole, *got = lax.optimization_barrier((whole, *got))
    return parts, got, whole


def places(y, z):
    sites = jnp.arange(16, dtype=jnp.int32)
    tables = []
    for order in ORDERS:
        off = {"y": (sites // 4) ^ y, "z": (sites % 4) ^ z}
        total = jnp.zeros_like(sites)
        for step, (axis, flip) in enumerate(order):
            o = off[axis]
            upper = o >> 1
            bit = upper if flip == 3 else (o & 1) ^ upper
            total = total + (bit << step)
        tables.append(total)
    return jnp.stack(tables).reshape(-1)


def split(value):
    high = value.astype(BF)
    return high, (value - high.astype(F32)).astype(BF)


def put_piece(factor_ref, base, out_ref):
    for u in range(12):
        rows = slice(base + u % 2 * 32, base + u % 2 * 32 + 32)
        at = 512 + u % 3 * 32
        out_ref[at:at + 32, u // 3 * 128:(u // 3 + 1) * 128] = factor_ref[rows, u // 2 * 128:(u // 2 + 1) * 128]


def load_kernel(rhs_ref, factor_ref, *outs):
    for d in range(4):
        for j in range(4):
            lanes = slice(j * 128, (j + 1) * 128)
            at = d * 512 + j * 128
            outs[d][:512, lanes] = rhs_ref[0, :, at:at + 128].astype(BF)
            at = j * 512 + d * 128
            outs[4 + d][:512, lanes] = split(rhs_ref[0, :, at:at + 128])[1]
        put_piece(factor_ref, d * 64, outs[d])
        put_piece(factor_ref, 256 + d * 64, outs[4 + d])


def loads(rhs, factor):
    return pl.pallas_call(
        load_kernel,
        grid=(1,),
        in_specs=[pl.BlockSpec((1, 512, 2048), lambda i: (0, 0, 0)), pl.BlockSpec((512, 1024), lambda i: (0, 0))],
        out_specs=[pl.BlockSpec((608, 512), lambda i: (0, 0))] * 8,
        out_shape=[jax.ShapeDtypeStruct((608, 512), BF)] * 8,
        compiler_params=pltpu.CompilerParams(vmem_limit_bytes=48 << 20),
    )(rhs, factor)


def solve(high_ref, low_ref, state):
    high, low = split(state)
    dot = lambda a, b: jnp.dot(a, b, preferred_element_type=F32)
    return (dot(high_ref[...], high) + dot(high_ref[...], low) + dot(low_ref[...], high)).astype(BF)


def first_kernel(scalars, state_ref, high_ref, low_ref, sent_ref):
    sent_ref[...] = solve(high_ref, low_ref, state_ref[...])


def step_kernel(panel, scalars, state_ref, high_ref, low_ref, mine_ref, other_ref, *refs):
    dot = lambda a, b: jnp.dot(a, b, preferred_element_type=F32)
    swap = scalars[0] == 1
    left = jnp.where(swap, other_ref[0], mine_ref[0])
    right = jnp.where(swap, mine_ref[0], other_ref[0])
    gots = refs[:3 - panel]
    got = sum(g[...] for g in gots)
    state = state_ref[...] - dot(left, got[:256]) - dot(right, got[256:])
    here = scalars[1] == panel
    if panel == 0:
        sent_ref, next_ref, new_ref, done_ref = refs[3:]
        done_ref[...] = jnp.where(here, sent_ref[...], got)
    elif panel == 1:
        sent_ref, back_ref, last_ref, next_ref, new_ref, done_ref = refs[2:]
        done_ref[:512] = last_ref[...]
        done_ref[512:] = jnp.where(here, sent_ref[...], got + back_ref[...])
    else:
        next_ref, new_ref = refs[1:]
    next_ref[...] = state
    new_ref[...] = solve(high_ref, low_ref, state)


def step(scalars, state, inverse, factor=None, panel=None, more=()):
    full = lambda shape: pl.BlockSpec(shape, lambda i, s: (0, 0))
    part = pl.BlockSpec((1, 512, 256), lambda i, s: (panel, 0, 0))
    tall, square = full((512, 128)), full((512, 512))
    shapes = [jax.ShapeDtypeStruct((512, 128), BF)]
    if panel is None:
        kernel, ins, factor = first_kernel, [], ()
    else:
        kernel, ins = lambda *refs: step_kernel(panel, *refs), [part, part] + [tall] * len(more)
        shapes = [jax.ShapeDtypeStruct((512, 128), F32)] + shapes
        if panel < 2:
            shapes.append(jax.ShapeDtypeStruct((512 * (panel + 1), 128), BF))
    return pl.pallas_call(
        kernel,
        grid_spec=pltpu.PrefetchScalarGridSpec(
            num_scalar_prefetch=1,
            grid=(1,),
            in_specs=[tall, square, square] + ins,
            out_specs=[full(v.shape) for v in shapes],
        ),
        out_shape=shapes,
        compiler_params=pltpu.CompilerParams(vmem_limit_bytes=32 << 20),
    )(scalars, state, *inverse, *factor, *more)


def update_kernel(scalars, factor_ref, rhs_ref, early_ref, *rest):
    near, far, out_ref, sent_ref = rest[:8], rest[8:16], rest[16], rest[17]
    j = pl.program_id(0)
    for h in range(2):
        lanes = slice(h * 128, (h + 1) * 128)
        sent_ref[:1024, lanes] = early_ref[h]
        for p in range(4):
            rows = slice(1024 + p * 256, 1280 + p * 256)
            low = scalars[p * 16 + 2 * j + h] < 8

            @pl.when(low)
            def _():
                sent_ref[rows, lanes] = near[p * 2 + h][0]

            @pl.when(jnp.logical_not(low))
            def _():
                sent_ref[rows, lanes] = far[p * 2 + h][0]
    for c in range(2):
        out_ref[c] = rhs_ref[c] - jnp.dot(factor_ref[c], sent_ref[...], preferred_element_type=F32)
    place = scalars[64]

    @pl.when(place < 4)
    def _():
        out_ref[0] = sent_ref[pl.ds(pl.multiple_of(place * 512, 512), 512), :].astype(F32)


def update(scalars, factor, rhs, early, near, far):
    cycles, tile, depth = factor.shape
    pairs = [(p, h) for p in range(4) for h in range(2)]
    near_specs = [
        pl.BlockSpec((1, 256, 128), lambda j, s, p=p, h=h: (jnp.minimum(s[p * 16 + 2 * j + h], 7), 0, 0))
        for p, h in pairs
    ]
    far_specs = [
        pl.BlockSpec((1, 256, 128), lambda j, s, p=p, h=h: (jnp.maximum(s[p * 16 + 2 * j + h] - 8, 0), 0, 0))
        for p, h in pairs
    ]
    return pl.pallas_call(
        update_kernel,
        grid_spec=pltpu.PrefetchScalarGridSpec(
            num_scalar_prefetch=1,
            grid=(rhs.shape[2] // 256,),
            in_specs=[
                pl.BlockSpec((cycles, tile, depth), lambda j, s: (0, 0, 0)),
                pl.BlockSpec((cycles, tile, 256), lambda j, s: (0, 0, j)),
                pl.BlockSpec((2, 1024, 128), lambda j, s: (j, 0, 0)),
            ] + near_specs + far_specs,
            out_specs=pl.BlockSpec((cycles, tile, 256), lambda j, s: (0, 0, j)),
            scratch_shapes=[pltpu.VMEM((depth, 256), BF)],
        ),
        out_shape=jax.ShapeDtypeStruct(rhs.shape, F32),
        compiler_params=pltpu.CompilerParams(vmem_limit_bytes=48 << 20),
    )(scalars, factor, rhs, early, *[near[p] for p, _ in pairs], *[far[p] for p, _ in pairs])


def local(rhs, factor, inverses):
    x, y, z = (lax.axis_index(a) for a in ("x", "y", "z"))
    core = lax.axis_index("rhs")
    place = (y * 4 + z) * 4 + x
    owner = place < 4
    zero = jnp.zeros((), BF)

    tile = factor[0].reshape(512, 1024)
    slabs = loads(rhs, tile)
    outward = {
        (p, d): permute(slabs[4 * p + d], [((i, 0, 0), (i, 0, d) if p else (i, d, 0)) for i in range(4)])
        for p, d in ((0, 3), (0, 1), (1, 1), (0, 2), (1, 2), (1, 3))
    }
    hold_a = jnp.where(owner, slabs[0], zero) + outward[0, 1] + outward[0, 2] + outward[0, 3]
    own_b, hold_a = lax.optimization_barrier((slabs[4], hold_a))
    hold_b = jnp.where(owner, own_b, zero) + outward[1, 1] + outward[1, 2] + outward[1, 3]

    def finish(hold, axis):
        tail = [hold[512:, k * 128:(k + 1) * 128] for k in range(4)]
        message = lambda d: jnp.concatenate([hold[:512, d * 128:(d + 1) * 128]] + tail, axis=0)
        mine = jnp.where((z if axis == "y" else y) == 0, message(0), zero)
        for d in (1, 3, 2):
            if axis == "y":
                moves = [((i, j, 0), (i, j, d)) for i in range(4) for j in range(4)]
            else:
                moves = [((i, 0, j), (i, d, j)) for i in range(4) for j in range(4)]
            mine = mine + permute(message(d), moves)
        return mine

    whole = lax.all_gather(factor, "rhs", axis=3, tiled=True)
    tiles = jnp.arange(2, dtype=jnp.int32) * 64 + place
    keep = tiles[:, None] > jnp.arange(4, dtype=jnp.int32)[None]
    whole = jnp.where(keep[:, None, :, None], whole, zero).reshape(2, 512, 2048)

    mine_a = finish(hold_a, "y")
    mine_b = finish(hold_b, "z")

    inverse = lax.dynamic_index_in_dim(inverses, x, 0, keepdims=False)
    rounded = lax.reduce_precision(inverse, 8, 7)
    inverse = (rounded.astype(BF), (inverse - rounded).astype(BF))
    where = jnp.stack([core, x]).astype(jnp.int32)
    state = mine_a[:512].astype(F32) + mine_b[:512].astype(F32)
    state, *inverse = lax.optimization_barrier((state, *inverse))
    sent_0, = step(where, state, inverse)
    gots = [hop(sent_0, (0, 1)), hop(sent_0, (0, 3)), hop(sent_0, (0, 2))]

    piece_a, piece_b, _ = lax.optimization_barrier((mine_a[512:], mine_b[512:], sent_0))
    top = ring_gather(piece_a, "y")
    bottom = ring_gather(piece_b, "z")
    half = jnp.concatenate([top, bottom], axis=0).reshape(8, 3, 2, 64, 128).transpose(1, 0, 3, 2, 4).reshape(3, 512, 256)
    half, *gots = lax.optimization_barrier((half, *gots))
    block = (half, lax.ppermute(half, "rhs", [(0, 1), (1, 0)]))

    state, sent_1, panel_0 = step(where, state, inverse, block, 0, (*gots, sent_0))
    gots = [hop(sent_1, (1, 2)), hop(sent_1, (1, 3))]
    back_1 = hop(sent_1, (1, 0))
    state, sent_2, pair = step(where, state, inverse, block, 1, (*gots, sent_1, back_1, panel_0))
    early = lax.all_gather(pair, ("y", "z"), axis=0)
    got = hop(sent_2, (2, 3))
    state, sent = step(where, state, inverse, block, 2, (got,))
    sent_2 = jnp.where(x == 2, sent_2, zero)
    sent = jnp.where(x == 3, sent, sent_2)
    back = hop(sent, (2, 1), (3, 2))
    far = hop(sent, (2, 0), (3, 1))
    wrap = hop(sent, (3, 0))
    panel_2 = jnp.where(x == 2, sent, jnp.where(x == 3, got, jnp.where(x == 1, back, far)))
    panel_3 = jnp.where(x == 3, sent, jnp.where(x == 2, back, jnp.where(x == 1, far, wrap)))
    near, far_late, whole = spread([panel_2[:256], panel_2[256:], panel_3[:256], panel_3[256:]], whole)

    scalars = jnp.concatenate([places(y, z), place[None]]).astype(jnp.int32)
    return update(scalars, whole, rhs, early, near, far_late)


def solution(mesh):
    grid = Mesh(mesh.devices.reshape(4, 4, 4, 2), ("y", "z", "x", "rhs"))
    return jax.shard_map(
        local,
        mesh=grid,
        in_specs=(P(None, ROWS, "rhs"), P(None, ROWS, None, "rhs"), P()),
        out_specs=P(None, ROWS, "rhs"),
        check_vma=False,
    )
```

```python
import jax
import jax.numpy as jnp
from jax import lax
from jax.experimental import pallas as pl
from jax.experimental.pallas import tpu as pltpu
from jax.sharding import Mesh, PartitionSpec as P

ROWS = ("y", "z", "x")
BF = jnp.bfloat16
F32 = jnp.float32
ALL = [(j, k) for j in range(4) for k in range(4)]
ORDERS = (
    (("y", 1), ("y", 3), ("z", 1), ("z", 3)),
    (("y", 3), ("y", 1), ("z", 3), ("z", 1)),
    (("z", 1), ("z", 3), ("y", 1), ("y", 3)),
    (("z", 3), ("z", 1), ("y", 3), ("y", 1)),
)


def flat(x, y, z):
    return ((y % 4) * 4 + (z % 4)) * 4 + (x % 4)


def permute(value, moves):
    return lax.ppermute(value, ROWS, [(flat(*a), flat(*b)) for a, b in moves])


def hop(value, *planes):
    return permute(value, [((a, j, k), (b, j, k)) for a, b in planes for j, k in ALL])


def swap(value, axis, flip):
    return lax.ppermute(value, axis, [(i, i ^ flip) for i in range(4)])


def spread(parts):
    parts = [p[None] for p in parts]
    for step in range(3):
        got = [swap(p, *order[step]) for p, order in zip(parts, ORDERS)]
        parts = [jnp.concatenate([p, g], axis=0) for p, g in zip(parts, got)]
    return parts, [swap(p, *order[3]) for p, order in zip(parts, ORDERS)]


def places(y, z):
    sites = jnp.arange(16, dtype=jnp.int32)
    tables = []
    for order in ORDERS:
        off = {"y": (sites // 4) ^ y, "z": (sites % 4) ^ z}
        total = jnp.zeros_like(sites)
        for step, (axis, flip) in enumerate(order):
            o = off[axis]
            upper = o >> 1
            bit = upper if flip == 3 else (o & 1) ^ upper
            total = total + (bit << step)
        tables.append(total)
    return jnp.stack(tables).reshape(-1)


def split(value):
    high = value.astype(BF)
    return high, (value - high.astype(F32)).astype(BF)


def put_piece(factor_ref, base, out_ref):
    for u in range(12):
        rows = slice(base + u % 2 * 32, base + u % 2 * 32 + 32)
        at = 512 + u % 3 * 32
        out_ref[at:at + 32, u // 3 * 128:(u // 3 + 1) * 128] = factor_ref[0, rows, u // 2 * 128:(u // 2 + 1) * 128]


def load_kernel(rhs_ref, factor_ref, *outs):
    for d in range(4):
        for j in range(4):
            lanes = slice(j * 128, (j + 1) * 128)
            at = d * 512 + j * 128
            outs[d][:512, lanes] = rhs_ref[0, :, at:at + 128].astype(BF)
            at = j * 512 + d * 128
            outs[4 + d][:512, lanes] = split(rhs_ref[0, :, at:at + 128])[1]
        put_piece(factor_ref, d * 64, outs[d])
        put_piece(factor_ref, 256 + d * 64, outs[4 + d])


def loads(rhs, factor):
    return pl.pallas_call(
        load_kernel,
        grid=(1,),
        in_specs=[pl.BlockSpec((1, 512, 2048), lambda i: (0, 0, 0)), pl.BlockSpec((1, 512, 1024), lambda i: (0, 0, 0))],
        out_specs=[pl.BlockSpec((608, 512), lambda i: (0, 0))] * 8,
        out_shape=[jax.ShapeDtypeStruct((608, 512), BF)] * 8,
        compiler_params=pltpu.CompilerParams(vmem_limit_bytes=48 << 20),
    )(rhs, factor)


def solve(high_ref, low_ref, state):
    high, low = split(state)
    dot = lambda a, b: jnp.dot(a, b, preferred_element_type=F32)
    return (dot(high_ref[...], high) + dot(high_ref[...], low) + dot(low_ref[...], high)).astype(BF)


def first_kernel(scalars, state_ref, high_ref, low_ref, sent_ref):
    sent_ref[...] = solve(high_ref, low_ref, state_ref[...])


def step_kernel(panel, scalars, state_ref, high_ref, low_ref, *refs):
    dot = lambda a, b: jnp.dot(a, b, preferred_element_type=F32)
    pieces, refs, block_ref = refs[:4], refs[4:-1], refs[-1]
    core = scalars[0]
    for source in range(2):
        half = core if source == 0 else 1 - core
        for side in range(2):
            for i in range(4):
                off = scalars[2 + side] ^ i
                at = off ^ (off >> 1)
                rows = slice(side * 256 + i * 64, side * 256 + i * 64 + 64)
                for h in range(2):
                    block_ref[half, rows, h * 128:(h + 1) * 128] = pieces[2 * source + side][at, 0, h * 64:(h + 1) * 64]
    gots = refs[:3 - panel]
    got = sum(g[...] for g in gots)
    state = state_ref[...] - dot(block_ref[0], got[:256]) - dot(block_ref[1], got[256:])
    here = scalars[1] == panel
    if panel == 0:
        sent_ref, next_ref, new_ref, done_ref = refs[3:]
        done_ref[...] = jnp.where(here, sent_ref[...], got)
    elif panel == 1:
        sent_ref, back_ref, last_ref, next_ref, new_ref, done_ref = refs[2:]
        done_ref[:512] = last_ref[...]
        done_ref[512:] = jnp.where(here, sent_ref[...], got + back_ref[...])
    else:
        next_ref, new_ref = refs[1:]
    next_ref[...] = state
    new_ref[...] = solve(high_ref, low_ref, state)


def step(scalars, state, inverse, factor=None, panel=None, more=()):
    full = lambda shape: pl.BlockSpec(shape, lambda i, s: (0, 0))
    part = pl.BlockSpec((4, 1, 128, 128), lambda i, s: (0, panel, 0, 0))
    tall, square = full((512, 128)), full((512, 512))
    shapes = [jax.ShapeDtypeStruct((512, 128), BF)]
    scratch = []
    if panel is None:
        kernel, ins, factor = first_kernel, [], ()
    else:
        kernel, ins = lambda *refs: step_kernel(panel, *refs), [part] * 4 + [tall] * len(more)
        scratch = [pltpu.VMEM((2, 512, 256), BF)]
        shapes = [jax.ShapeDtypeStruct((512, 128), F32)] + shapes
        if panel < 2:
            shapes.append(jax.ShapeDtypeStruct((512 * (panel + 1), 128), BF))
    return pl.pallas_call(
        kernel,
        grid_spec=pltpu.PrefetchScalarGridSpec(
            num_scalar_prefetch=1,
            grid=(1,),
            in_specs=[tall, square, square] + ins,
            out_specs=[full(v.shape) for v in shapes],
            scratch_shapes=scratch,
        ),
        out_shape=shapes,
        compiler_params=pltpu.CompilerParams(vmem_limit_bytes=32 << 20),
    )(scalars, state, *inverse, *factor, *more)


def update_kernel(scalars, mine_ref, other_ref, rhs_ref, early_ref, *rest):
    near, far, out_ref, sent_ref = rest[:8], rest[8:16], rest[16], rest[17]
    j = pl.program_id(0)
    place, core = scalars[64], scalars[65]

    def rows(panel, half):
        return pl.ds(pl.multiple_of((core ^ half) * 1024 + panel * 256, 256), 256)

    for h in range(2):
        lanes = slice(h * 128, (h + 1) * 128)
        for p in range(4):
            sent_ref[rows(p // 2, p % 2), lanes] = early_ref[h, p * 256:(p + 1) * 256]
            low = scalars[p * 16 + 2 * j + h] < 8

            @pl.when(low)
            def _():
                sent_ref[rows(2 + p // 2, p % 2), lanes] = near[p * 2 + h][0]

            @pl.when(jnp.logical_not(low))
            def _():
                sent_ref[rows(2 + p // 2, p % 2), lanes] = far[p * 2 + h][0]
    dot = lambda a, b: jnp.dot(a, b, preferred_element_type=F32)
    for c in range(2):
        out_ref[c] = rhs_ref[c] - (dot(mine_ref[c], sent_ref[:1024]) + dot(other_ref[c], sent_ref[1024:]))

    @pl.when(place < 4)
    def _():
        for half in range(2):
            out_ref[0, half * 256:(half + 1) * 256] = sent_ref[rows(place, half), :].astype(F32)


def update(scalars, mine, other, rhs, early, near, far):
    cycles, tile, depth = mine.shape
    pairs = [(p, h) for p in range(4) for h in range(2)]
    near_specs = [
        pl.BlockSpec((1, 256, 128), lambda j, s, p=p, h=h: (jnp.minimum(s[p * 16 + 2 * j + h], 7), 0, 0))
        for p, h in pairs
    ]
    far_specs = [
        pl.BlockSpec((1, 256, 128), lambda j, s, p=p, h=h: (jnp.maximum(s[p * 16 + 2 * j + h] - 8, 0), 0, 0))
        for p, h in pairs
    ]
    return pl.pallas_call(
        update_kernel,
        grid_spec=pltpu.PrefetchScalarGridSpec(
            num_scalar_prefetch=1,
            grid=(rhs.shape[2] // 256,),
            in_specs=[
                pl.BlockSpec((cycles, tile, depth), lambda j, s: (0, 0, 0)),
                pl.BlockSpec((cycles, tile, depth), lambda j, s: (0, 0, 0)),
                pl.BlockSpec((cycles, tile, 256), lambda j, s: (0, 0, j)),
                pl.BlockSpec((2, 1024, 128), lambda j, s: (j, 0, 0)),
            ] + near_specs + far_specs,
            out_specs=pl.BlockSpec((cycles, tile, 256), lambda j, s: (0, 0, j)),
            scratch_shapes=[pltpu.VMEM((2 * depth, 256), BF)],
        ),
        out_shape=jax.ShapeDtypeStruct(rhs.shape, F32),
        compiler_params=pltpu.CompilerParams(vmem_limit_bytes=48 << 20),
    )(scalars, mine, other, rhs, early, *[near[p] for p, _ in pairs], *[far[p] for p, _ in pairs])


def local(rhs, factor, inverses):
    x, y, z = (lax.axis_index(a) for a in ("x", "y", "z"))
    core = lax.axis_index("rhs")
    place = (y * 4 + z) * 4 + x
    owner = place < 4
    zero = jnp.zeros((), BF)

    flat_factor = factor.reshape(2, 512, 1024)
    other_factor = lax.ppermute(flat_factor, "rhs", [(0, 1), (1, 0)])
    slabs = loads(rhs, flat_factor)
    outward = {
        (p, d): permute(slabs[4 * p + d], [((i, 0, 0), (i, 0, d) if p else (i, d, 0)) for i in range(4)])
        for p, d in ((0, 3), (0, 1), (1, 1), (0, 2), (1, 2), (1, 3))
    }
    hold_a = jnp.where(owner, slabs[0], zero) + outward[0, 1] + outward[0, 2] + outward[0, 3]
    own_b, hold_a = lax.optimization_barrier((slabs[4], hold_a))
    hold_b = jnp.where(owner, own_b, zero) + outward[1, 1] + outward[1, 2] + outward[1, 3]

    def finish(hold, axis):
        tail = [hold[512:, k * 128:(k + 1) * 128] for k in range(4)]
        message = lambda d: jnp.concatenate([hold[:512, d * 128:(d + 1) * 128]] + tail, axis=0)
        mine = jnp.where((z if axis == "y" else y) == 0, message(0), zero)
        for d in (1, 3, 2):
            if axis == "y":
                moves = [((i, j, 0), (i, j, d)) for i in range(4) for j in range(4)]
            else:
                moves = [((i, 0, j), (i, d, j)) for i in range(4) for j in range(4)]
            mine = mine + permute(message(d), moves)
        return mine

    mine_a = finish(hold_a, "y")
    mine_b = finish(hold_b, "z")

    inverse = lax.dynamic_index_in_dim(inverses, x, 0, keepdims=False)
    rounded = lax.reduce_precision(inverse, 8, 7)
    inverse = (rounded.astype(BF), (inverse - rounded).astype(BF))
    where = jnp.stack([core, x, y, z]).astype(jnp.int32)
    state = mine_a[:512].astype(F32) + mine_b[:512].astype(F32)
    state, *inverse = lax.optimization_barrier((state, *inverse))
    sent_0, = step(where, state, inverse)
    gots = [hop(sent_0, (0, 1)), hop(sent_0, (0, 3)), hop(sent_0, (0, 2))]

    piece_a, piece_b, _ = lax.optimization_barrier((mine_a[512:], mine_b[512:], sent_0))
    near_a, near_b = swap(piece_a, "y", 1), swap(piece_b, "z", 1)
    near_a, near_b, *gots = lax.optimization_barrier((near_a, near_b, *gots))

    def complete(piece, near, axis):
        two = jnp.stack([piece, near])
        return jnp.concatenate([two, swap(two, axis, 3)], axis=0).reshape(4, 3, 128, 128)

    top, bottom = complete(piece_a, near_a, "y"), complete(piece_b, near_b, "z")
    block = (top, bottom, lax.ppermute(top, "rhs", [(0, 1), (1, 0)]), lax.ppermute(bottom, "rhs", [(0, 1), (1, 0)]))

    state, sent_1, panel_0 = step(where, state, inverse, block, 0, (*gots, sent_0))
    gots = [hop(sent_1, (1, 2)), hop(sent_1, (1, 3))]
    back_1 = hop(sent_1, (1, 0))
    state, sent_2, pair = step(where, state, inverse, block, 1, (*gots, sent_1, back_1, panel_0))
    early = lax.all_gather(pair, ("y", "z"), axis=0)
    got = hop(sent_2, (2, 3))
    state, sent = step(where, state, inverse, block, 2, (got,))
    sent_2 = jnp.where(x == 2, sent_2, zero)
    sent = jnp.where(x == 3, sent, sent_2)
    back = hop(sent, (2, 1), (3, 2))
    far = hop(sent, (2, 0), (3, 1))
    wrap = hop(sent, (3, 0))
    panel_2 = jnp.where(x == 2, sent, jnp.where(x == 3, got, jnp.where(x == 1, back, far)))
    panel_3 = jnp.where(x == 3, sent, jnp.where(x == 2, back, jnp.where(x == 1, far, wrap)))
    near, far_late = spread([panel_2[:256], panel_2[256:], panel_3[:256], panel_3[256:]])

    scalars = jnp.concatenate([places(y, z), jnp.stack([place, core])]).astype(jnp.int32)
    return update(scalars, flat_factor, other_factor, rhs, early, near, far_late)


def solution(mesh):
    grid = Mesh(mesh.devices.reshape(4, 4, 4, 2), ("y", "z", "x", "rhs"))
    return jax.shard_map(
        local,
        mesh=grid,
        in_specs=(P(None, ROWS, "rhs"), P(None, ROWS, None, "rhs"), P()),
        out_specs=P(None, ROWS, "rhs"),
        check_vma=False,
    )
```

```python
import jax
import jax.numpy as jnp
from jax import lax
from jax.experimental import pallas as pl
from jax.experimental.pallas import tpu as pltpu
from jax.sharding import Mesh, PartitionSpec as P

ROWS = ("y", "z", "x")
BF = jnp.bfloat16
F32 = jnp.float32
ALL = [(j, k) for j in range(4) for k in range(4)]
ORDERS = (
    (("y", 1), ("y", 3), ("z", 1), ("z", 3)),
    (("y", 3), ("y", 1), ("z", 3), ("z", 1)),
    (("z", 1), ("z", 3), ("y", 1), ("y", 3)),
    (("z", 3), ("z", 1), ("y", 3), ("y", 1)),
)


def flat(x, y, z):
    return ((y % 4) * 4 + (z % 4)) * 4 + (x % 4)


def permute(value, moves):
    return lax.ppermute(value, ROWS, [(flat(*a), flat(*b)) for a, b in moves])


def hop(value, *planes):
    return permute(value, [((a, j, k), (b, j, k)) for a, b in planes for j, k in ALL])


def swap(value, axis, flip):
    return lax.ppermute(value, axis, [(i, i ^ flip) for i in range(4)])


def spread(parts, factor):
    parts = [p[None] for p in parts]
    for step in range(3):
        got = [swap(p, *order[step]) for p, order in zip(parts, ORDERS)]
        if step == 1:
            factor, *got = lax.optimization_barrier((factor, *got))
        parts = [jnp.concatenate([p, g], axis=0) for p, g in zip(parts, got)]
    return parts, factor, [swap(p, *order[3]) for p, order in zip(parts, ORDERS)]


def places(y, z):
    sites = jnp.arange(16, dtype=jnp.int32)
    tables = []
    for order in ORDERS:
        off = {"y": (sites // 4) ^ y, "z": (sites % 4) ^ z}
        total = jnp.zeros_like(sites)
        for step, (axis, flip) in enumerate(order):
            o = off[axis]
            upper = o >> 1
            bit = upper if flip == 3 else (o & 1) ^ upper
            total = total + (bit << step)
        tables.append(total)
    return jnp.stack(tables).reshape(-1)


def split(value):
    high = value.astype(BF)
    return high, (value - high.astype(F32)).astype(BF)


def put_piece(factor_ref, base, out_ref):
    for u in range(12):
        rows = slice(base + u % 2 * 32, base + u % 2 * 32 + 32)
        at = 512 + u % 3 * 32
        out_ref[at:at + 32, u // 3 * 128:(u // 3 + 1) * 128] = factor_ref[0, rows, u // 2 * 128:(u // 2 + 1) * 128]


def load_kernel(rhs_ref, factor_ref, *outs):
    for d in range(4):
        for j in range(4):
            lanes = slice(j * 128, (j + 1) * 128)
            at = d * 512 + j * 128
            outs[d][:512, lanes] = rhs_ref[0, :, at:at + 128].astype(BF)
            at = j * 512 + d * 128
            outs[4 + d][:512, lanes] = split(rhs_ref[0, :, at:at + 128])[1]
        put_piece(factor_ref, d * 64, outs[d])
        put_piece(factor_ref, 256 + d * 64, outs[4 + d])


def loads(rhs, factor):
    return pl.pallas_call(
        load_kernel,
        grid=(1,),
        in_specs=[pl.BlockSpec((1, 512, 2048), lambda i: (0, 0, 0)), pl.BlockSpec((1, 512, 1024), lambda i: (0, 0, 0))],
        out_specs=[pl.BlockSpec((608, 512), lambda i: (0, 0))] * 8,
        out_shape=[jax.ShapeDtypeStruct((608, 512), BF)] * 8,
        compiler_params=pltpu.CompilerParams(vmem_limit_bytes=48 << 20),
    )(rhs, factor)


def solve(high_ref, low_ref, state):
    high, low = split(state)
    dot = lambda a, b: jnp.dot(a, b, preferred_element_type=F32)
    return (dot(high_ref[...], high) + dot(high_ref[...], low) + dot(low_ref[...], high)).astype(BF)


def first_kernel(scalars, state_ref, high_ref, low_ref, sent_ref):
    sent_ref[...] = solve(high_ref, low_ref, state_ref[...])


def step_kernel(panel, scalars, state_ref, high_ref, low_ref, *refs):
    dot = lambda a, b: jnp.dot(a, b, preferred_element_type=F32)
    pieces, refs, block_ref = refs[:4], refs[4:-1], refs[-1]
    core = scalars[0]
    for source in range(2):
        half = core if source == 0 else 1 - core
        for side in range(2):
            for i in range(4):
                off = scalars[2 + side] ^ i
                at = off ^ (off >> 1)
                rows = slice(side * 256 + i * 64, side * 256 + i * 64 + 64)
                for h in range(2):
                    block_ref[half, rows, h * 128:(h + 1) * 128] = pieces[2 * source + side][at, 0, h * 64:(h + 1) * 64]
    gots = refs[:3 - panel]
    got = sum(g[...] for g in gots)
    state = state_ref[...] - dot(block_ref[0], got[:256]) - dot(block_ref[1], got[256:])
    if panel == 1:
        sent_ref, back_ref, next_ref, new_ref, done_ref = refs[2:]
        done_ref[...] = jnp.where(scalars[1] == 1, sent_ref[...], got + back_ref[...])
    else:
        next_ref, new_ref = refs[3 - panel:]
    next_ref[...] = state
    new_ref[...] = solve(high_ref, low_ref, state)


def step(scalars, state, inverse, factor=None, panel=None, more=()):
    full = lambda shape: pl.BlockSpec(shape, lambda i, s: (0, 0))
    part = pl.BlockSpec((4, 1, 128, 128), lambda i, s: (0, panel, 0, 0))
    tall, square = full((512, 128)), full((512, 512))
    shapes = [jax.ShapeDtypeStruct((512, 128), BF)]
    scratch = []
    if panel is None:
        kernel, ins, factor = first_kernel, [], ()
    else:
        kernel, ins = lambda *refs: step_kernel(panel, *refs), [part] * 4 + [tall] * len(more)
        scratch = [pltpu.VMEM((2, 512, 256), BF)]
        shapes = [jax.ShapeDtypeStruct((512, 128), F32)] + shapes
        if panel == 1:
            shapes.append(jax.ShapeDtypeStruct((512, 128), BF))
    return pl.pallas_call(
        kernel,
        grid_spec=pltpu.PrefetchScalarGridSpec(
            num_scalar_prefetch=1,
            grid=(1,),
            in_specs=[tall, square, square] + ins,
            out_specs=[full(v.shape) for v in shapes],
            scratch_shapes=scratch,
        ),
        out_shape=shapes,
        compiler_params=pltpu.CompilerParams(vmem_limit_bytes=32 << 20),
    )(scalars, state, *inverse, *factor, *more)


def begin_kernel(scalars, mine_ref, other_ref, rhs_ref, early_ref, out_ref, sent_ref):
    place, core = scalars[64], scalars[65]
    for h in range(2):
        sent_ref[:, h * 128:(h + 1) * 128] = early_ref[h]
    dot = lambda a, b: jnp.dot(a, b, preferred_element_type=F32)
    near = sent_ref[pl.ds(pl.multiple_of(core * 256, 256), 256), :]
    far = sent_ref[pl.ds(pl.multiple_of(256 - core * 256, 256), 256), :]
    for c in range(2):
        out_ref[c] = rhs_ref[c] - (dot(mine_ref[c], near) + dot(other_ref[c], far))

    @pl.when(place == 0)
    def _():
        out_ref[0] = sent_ref[...].astype(F32)


def begin(scalars, mine, other, rhs, early):
    block = pl.BlockSpec((2, 512, 256), lambda j, s: (0, 0, j))
    fixed = pl.BlockSpec((2, 512, 256), lambda j, s: (0, 0, 0))
    return pl.pallas_call(
        begin_kernel,
        grid_spec=pltpu.PrefetchScalarGridSpec(
            num_scalar_prefetch=1,
            grid=(rhs.shape[2] // 256,),
            in_specs=[fixed, fixed, block, pl.BlockSpec((2, 512, 128), lambda j, s: (j, 0, 0))],
            out_specs=block,
            scratch_shapes=[pltpu.VMEM((512, 256), BF)],
        ),
        out_shape=jax.ShapeDtypeStruct(rhs.shape, F32),
        compiler_params=pltpu.CompilerParams(vmem_limit_bytes=48 << 20),
    )(scalars, mine, other, rhs, early)


def update_kernel(scalars, mine_ref, other_ref, rhs_ref, early_ref, *rest):
    near, far, out_ref, sent_ref = rest[:8], rest[8:16], rest[16], rest[17]
    j = pl.program_id(0)
    place, core = scalars[64], scalars[65]

    def rows(panel, half):
        return pl.ds(pl.multiple_of((core ^ half) * 768 + (panel - 1) * 256, 256), 256)

    for h in range(2):
        lanes = slice(h * 128, (h + 1) * 128)
        for half in range(2):
            sent_ref[rows(1, half), lanes] = early_ref[h, half * 256:(half + 1) * 256]
        for p in range(4):
            low = scalars[p * 16 + 2 * j + h] < 8

            @pl.when(low)
            def _():
                sent_ref[rows(2 + p // 2, p % 2), lanes] = near[p * 2 + h][0]

            @pl.when(jnp.logical_not(low))
            def _():
                sent_ref[rows(2 + p // 2, p % 2), lanes] = far[p * 2 + h][0]
    dot = lambda a, b: jnp.dot(a, b, preferred_element_type=F32)
    for c in range(2):
        product = dot(mine_ref[c, :, 256:], sent_ref[:768]) + dot(other_ref[c, :, 256:], sent_ref[768:])
        out_ref[c] = rhs_ref[c] - product

    @pl.when(place == 0)
    def _():
        out_ref[0] = rhs_ref[0]

    @pl.when(jnp.logical_and(place > 0, place < 4))
    def _():
        for half in range(2):
            out_ref[0, half * 256:(half + 1) * 256] = sent_ref[rows(place, half), :].astype(F32)


def update(scalars, mine, other, rhs, early, near, far):
    cycles, tile, depth = mine.shape
    pairs = [(p, h) for p in range(4) for h in range(2)]
    near_specs = [
        pl.BlockSpec((1, 256, 128), lambda j, s, p=p, h=h: (jnp.minimum(s[p * 16 + 2 * j + h], 7), 0, 0))
        for p, h in pairs
    ]
    far_specs = [
        pl.BlockSpec((1, 256, 128), lambda j, s, p=p, h=h: (jnp.maximum(s[p * 16 + 2 * j + h] - 8, 0), 0, 0))
        for p, h in pairs
    ]
    return pl.pallas_call(
        update_kernel,
        grid_spec=pltpu.PrefetchScalarGridSpec(
            num_scalar_prefetch=1,
            grid=(rhs.shape[2] // 256,),
            in_specs=[
                pl.BlockSpec((cycles, tile, depth), lambda j, s: (0, 0, 0)),
                pl.BlockSpec((cycles, tile, depth), lambda j, s: (0, 0, 0)),
                pl.BlockSpec((cycles, tile, 256), lambda j, s: (0, 0, j)),
                pl.BlockSpec((2, 512, 128), lambda j, s: (j, 0, 0)),
            ] + near_specs + far_specs,
            out_specs=pl.BlockSpec((cycles, tile, 256), lambda j, s: (0, 0, j)),
            scratch_shapes=[pltpu.VMEM((1536, 256), BF)],
        ),
        out_shape=jax.ShapeDtypeStruct(rhs.shape, F32),
        compiler_params=pltpu.CompilerParams(vmem_limit_bytes=48 << 20),
    )(scalars, mine, other, rhs, early, *[near[p] for p, _ in pairs], *[far[p] for p, _ in pairs])


def local(rhs, factor, inverses):
    x, y, z = (lax.axis_index(a) for a in ("x", "y", "z"))
    core = lax.axis_index("rhs")
    place = (y * 4 + z) * 4 + x
    owner = place < 4
    zero = jnp.zeros((), BF)

    slabs = loads(rhs, factor[0].reshape(1, 512, 1024))
    outward = {
        (p, d): permute(slabs[4 * p + d], [((i, 0, 0), (i, 0, d) if p else (i, d, 0)) for i in range(4)])
        for p, d in ((0, 3), (0, 1), (1, 1), (0, 2), (1, 2), (1, 3))
    }
    hold_a = jnp.where(owner, slabs[0], zero) + outward[0, 1] + outward[0, 2] + outward[0, 3]
    own_b, hold_a = lax.optimization_barrier((slabs[4], hold_a))
    hold_b = jnp.where(owner, own_b, zero) + outward[1, 1] + outward[1, 2] + outward[1, 3]

    def finish(hold, axis):
        tail = [hold[512:, k * 128:(k + 1) * 128] for k in range(4)]
        message = lambda d: jnp.concatenate([hold[:512, d * 128:(d + 1) * 128]] + tail, axis=0)
        mine = jnp.where((z if axis == "y" else y) == 0, message(0), zero)
        for d in (1, 3, 2):
            if axis == "y":
                moves = [((i, j, 0), (i, j, d)) for i in range(4) for j in range(4)]
            else:
                moves = [((i, 0, j), (i, d, j)) for i in range(4) for j in range(4)]
            mine = mine + permute(message(d), moves)
        return mine

    mine_a = finish(hold_a, "y")
    mine_b = finish(hold_b, "z")

    inverse = lax.dynamic_index_in_dim(inverses, x, 0, keepdims=False)
    rounded = lax.reduce_precision(inverse, 8, 7)
    inverse = (rounded.astype(BF), (inverse - rounded).astype(BF))
    where = jnp.stack([core, x, y, z]).astype(jnp.int32)
    state = mine_a[:512].astype(F32) + mine_b[:512].astype(F32)
    state, *inverse = lax.optimization_barrier((state, *inverse))
    sent_0, = step(where, state, inverse)
    gots = [hop(sent_0, (0, 1)), hop(sent_0, (0, 3)), hop(sent_0, (0, 2))]

    piece_a, piece_b, _ = lax.optimization_barrier((mine_a[512:], mine_b[512:], sent_0))
    near_a, near_b = swap(piece_a, "y", 1), swap(piece_b, "z", 1)
    near_a, near_b, *gots = lax.optimization_barrier((near_a, near_b, *gots))

    def complete(piece, near, axis):
        two = jnp.stack([piece, near])
        return jnp.concatenate([two, swap(two, axis, 3)], axis=0).reshape(4, 3, 128, 128)

    top, bottom = complete(piece_a, near_a, "y"), complete(piece_b, near_b, "z")
    block = (top, bottom, lax.ppermute(top, "rhs", [(0, 1), (1, 0)]), lax.ppermute(bottom, "rhs", [(0, 1), (1, 0)]))

    panel_0 = jnp.where(x == 0, sent_0, gots[0] + gots[1] + gots[2])
    early_0 = lax.all_gather(panel_0, ("y", "z"), axis=0)
    state, sent_1 = step(where, state, inverse, block, 0, gots)
    gots = [hop(sent_1, (1, 2)), hop(sent_1, (1, 3))]
    back_1 = hop(sent_1, (1, 0))
    state, sent_2, panel_1 = step(where, state, inverse, block, 1, (*gots, sent_1, back_1))
    early_1 = lax.all_gather(panel_1, ("y", "z"), axis=0)
    got = hop(sent_2, (2, 3))
    state, sent = step(where, state, inverse, block, 2, (got,))
    sent_2 = jnp.where(x == 2, sent_2, zero)
    sent = jnp.where(x == 3, sent, sent_2)
    back = hop(sent, (2, 1), (3, 2))
    far = hop(sent, (2, 0), (3, 1))
    wrap = hop(sent, (3, 0))
    panel_2 = jnp.where(x == 2, sent, jnp.where(x == 3, got, jnp.where(x == 1, back, far)))
    panel_3 = jnp.where(x == 3, sent, jnp.where(x == 2, back, jnp.where(x == 1, far, wrap)))
    parts = [panel_2[:256], panel_2[256:], panel_3[:256], panel_3[256:]]
    near, flat_factor, far_late = spread(parts, factor.reshape(2, 512, 1024))
    other_factor = lax.ppermute(flat_factor, "rhs", [(0, 1), (1, 0)])

    scalars = jnp.concatenate([places(y, z), jnp.stack([place, core])]).astype(jnp.int32)
    begun = begin(scalars, flat_factor, other_factor, rhs, early_0)
    begun, *far_late = lax.optimization_barrier((begun, *far_late))
    return update(scalars, flat_factor, other_factor, begun, early_1, near, far_late)


def solution(mesh):
    grid = Mesh(mesh.devices.reshape(4, 4, 4, 2), ("y", "z", "x", "rhs"))
    return jax.shard_map(
        local,
        mesh=grid,
        in_specs=(P(None, ROWS, "rhs"), P(None, ROWS, None, "rhs"), P()),
        out_specs=P(None, ROWS, "rhs"),
        check_vma=False,
    )
```

```python
import jax
import jax.numpy as jnp
from jax import lax
from jax.experimental import pallas as pl
from jax.experimental.pallas import tpu as pltpu
from jax.sharding import Mesh, PartitionSpec as P

ROWS = ("y", "z", "x")
BF = jnp.bfloat16
F32 = jnp.float32
ALL = [(j, k) for j in range(4) for k in range(4)]
ORDERS = (
    (("y", 1), ("y", 3), ("z", 1), ("z", 3)),
    (("y", 3), ("y", 1), ("z", 3), ("z", 1)),
    (("z", 1), ("z", 3), ("y", 1), ("y", 3)),
    (("z", 3), ("z", 1), ("y", 3), ("y", 1)),
)


def flat(x, y, z):
    return ((y % 4) * 4 + (z % 4)) * 4 + (x % 4)


def permute(value, moves):
    return lax.ppermute(value, ROWS, [(flat(*a), flat(*b)) for a, b in moves])


def hop(value, *planes):
    return permute(value, [((a, j, k), (b, j, k)) for a, b in planes for j, k in ALL])


def swap(value, axis, flip):
    return lax.ppermute(value, axis, [(i, i ^ flip) for i in range(4)])


def spread(parts, factor, early):
    parts = [p[None] for p in parts]
    for step in range(3):
        got = [swap(p, *order[step]) for p, order in zip(parts, ORDERS)]
        if step == 0:
            early, *got = lax.optimization_barrier((early, *got))
        if step == 1:
            factor, *got = lax.optimization_barrier((factor, *got))
        parts = [jnp.concatenate([p, g], axis=0) for p, g in zip(parts, got)]
    return parts, factor, early, [swap(p, *order[3]) for p, order in zip(parts, ORDERS)]


def places(y, z):
    sites = jnp.arange(16, dtype=jnp.int32)
    tables = []
    for order in ORDERS:
        off = {"y": (sites // 4) ^ y, "z": (sites % 4) ^ z}
        total = jnp.zeros_like(sites)
        for step, (axis, flip) in enumerate(order):
            o = off[axis]
            upper = o >> 1
            bit = upper if flip == 3 else (o & 1) ^ upper
            total = total + (bit << step)
        tables.append(total)
    return jnp.stack(tables).reshape(-1)


def split(value):
    high = value.astype(BF)
    return high, (value - high.astype(F32)).astype(BF)


def put_piece(factor_ref, base, out_ref):
    for u in range(12):
        rows = slice(base + u % 2 * 32, base + u % 2 * 32 + 32)
        at = 512 + u % 3 * 32
        out_ref[at:at + 32, u // 3 * 128:(u // 3 + 1) * 128] = factor_ref[0, rows, u // 2 * 128:(u // 2 + 1) * 128]


def load_kernel(rhs_ref, factor_ref, *outs):
    for d in range(4):
        for j in range(4):
            lanes = slice(j * 128, (j + 1) * 128)
            at = d * 512 + j * 128
            outs[d][:512, lanes] = rhs_ref[0, :, at:at + 128].astype(BF)
            at = j * 512 + d * 128
            outs[4 + d][:512, lanes] = split(rhs_ref[0, :, at:at + 128])[1]
        put_piece(factor_ref, d * 64, outs[d])
        put_piece(factor_ref, 256 + d * 64, outs[4 + d])


def loads(rhs, factor):
    return pl.pallas_call(
        load_kernel,
        grid=(1,),
        in_specs=[pl.BlockSpec((1, 512, 2048), lambda i: (0, 0, 0)), pl.BlockSpec((1, 512, 1024), lambda i: (0, 0, 0))],
        out_specs=[pl.BlockSpec((608, 512), lambda i: (0, 0))] * 8,
        out_shape=[jax.ShapeDtypeStruct((608, 512), BF)] * 8,
        compiler_params=pltpu.CompilerParams(vmem_limit_bytes=48 << 20),
    )(rhs, factor)


def solve(high_ref, low_ref, state):
    high, low = split(state)
    dot = lambda a, b: jnp.dot(a, b, preferred_element_type=F32)
    return (dot(high_ref[...], high) + dot(high_ref[...], low) + dot(low_ref[...], high)).astype(BF)


def first_kernel(scalars, state_ref, high_ref, low_ref, sent_ref):
    sent_ref[...] = solve(high_ref, low_ref, state_ref[...])


def step_kernel(panel, scalars, state_ref, high_ref, low_ref, *refs):
    dot = lambda a, b: jnp.dot(a, b, preferred_element_type=F32)
    pieces, refs, block_ref = refs[:4], refs[4:-1], refs[-1]
    core = scalars[0]
    for source in range(2):
        half = core if source == 0 else 1 - core
        for side in range(2):
            for i in range(4):
                off = scalars[2 + side] ^ i
                at = off ^ (off >> 1)
                rows = slice(side * 256 + i * 64, side * 256 + i * 64 + 64)
                for h in range(2):
                    block_ref[half, rows, h * 128:(h + 1) * 128] = pieces[2 * source + side][at, 0, h * 64:(h + 1) * 64]
    gots = refs[:3 - panel]
    got = sum(g[...] for g in gots)
    state = state_ref[...] - dot(block_ref[0], got[:256]) - dot(block_ref[1], got[256:])
    next_ref, new_ref = refs[3 - panel:]
    next_ref[...] = state
    new_ref[...] = solve(high_ref, low_ref, state)


def step(scalars, state, inverse, factor=None, panel=None, more=()):
    full = lambda shape: pl.BlockSpec(shape, lambda i, s: (0, 0))
    part = pl.BlockSpec((4, 1, 128, 128), lambda i, s: (0, panel, 0, 0))
    tall, square = full((512, 128)), full((512, 512))
    shapes = [jax.ShapeDtypeStruct((512, 128), BF)]
    scratch = []
    if panel is None:
        kernel, ins, factor = first_kernel, [], ()
    else:
        kernel, ins = lambda *refs: step_kernel(panel, *refs), [part] * 4 + [tall] * len(more)
        scratch = [pltpu.VMEM((2, 512, 256), BF)]
        shapes = [jax.ShapeDtypeStruct((512, 128), F32)] + shapes
    return pl.pallas_call(
        kernel,
        grid_spec=pltpu.PrefetchScalarGridSpec(
            num_scalar_prefetch=1,
            grid=(1,),
            in_specs=[tall, square, square] + ins,
            out_specs=[full(v.shape) for v in shapes],
            scratch_shapes=scratch,
        ),
        out_shape=shapes,
        compiler_params=pltpu.CompilerParams(vmem_limit_bytes=32 << 20),
    )(scalars, state, *inverse, *factor, *more)


def update_kernel(scalars, mine_ref, other_ref, rhs_ref, early_ref, *rest):
    near, far, out_ref, sent_ref = rest[:8], rest[8:16], rest[16], rest[17]
    j = pl.program_id(0)
    place, core = scalars[64], scalars[65]

    def rows(panel, half, size=256):
        return pl.ds(pl.multiple_of((core ^ (half // 256)) * 1024 + panel * 256 + half % 256, 128), size)

    def put(part_ref, p, lanes):
        for u in range(3):
            row = 512 + p * 384 + u * 128
            sent_ref[rows(row // 512, row % 512, 128), lanes] = part_ref[0, u * 128:(u + 1) * 128]

    for h in range(2):
        lanes = slice(h * 128, (h + 1) * 128)
        for half in (0, 256):
            sent_ref[rows(0, half), lanes] = early_ref[h, half:half + 256]
        for p in range(4):
            low = scalars[p * 16 + 2 * j + h] < 8

            @pl.when(low)
            def _():
                put(near[p * 2 + h], p, lanes)

            @pl.when(jnp.logical_not(low))
            def _():
                put(far[p * 2 + h], p, lanes)
    dot = lambda a, b: jnp.dot(a, b, preferred_element_type=F32)
    for c in range(2):
        out_ref[c] = rhs_ref[c] - (dot(mine_ref[c], sent_ref[:1024]) + dot(other_ref[c], sent_ref[1024:]))

    @pl.when(place < 4)
    def _():
        for half in (0, 256):
            out_ref[0, half:half + 256] = sent_ref[rows(place, half), :].astype(F32)


def update(scalars, mine, other, rhs, early, near, far):
    cycles, tile, depth = mine.shape
    pairs = [(p, h) for p in range(4) for h in range(2)]
    near_specs = [
        pl.BlockSpec((1, 384, 128), lambda j, s, p=p, h=h: (jnp.minimum(s[p * 16 + 2 * j + h], 7), 0, 0))
        for p, h in pairs
    ]
    far_specs = [
        pl.BlockSpec((1, 384, 128), lambda j, s, p=p, h=h: (jnp.maximum(s[p * 16 + 2 * j + h] - 8, 0), 0, 0))
        for p, h in pairs
    ]
    return pl.pallas_call(
        update_kernel,
        grid_spec=pltpu.PrefetchScalarGridSpec(
            num_scalar_prefetch=1,
            grid=(rhs.shape[2] // 256,),
            in_specs=[
                pl.BlockSpec((cycles, tile, depth), lambda j, s: (0, 0, 0)),
                pl.BlockSpec((cycles, tile, depth), lambda j, s: (0, 0, 0)),
                pl.BlockSpec((cycles, tile, 256), lambda j, s: (0, 0, j)),
                pl.BlockSpec((2, 512, 128), lambda j, s: (j, 0, 0)),
            ] + near_specs + far_specs,
            out_specs=pl.BlockSpec((cycles, tile, 256), lambda j, s: (0, 0, j)),
            scratch_shapes=[pltpu.VMEM((2048, 256), BF)],
        ),
        out_shape=jax.ShapeDtypeStruct(rhs.shape, F32),
        compiler_params=pltpu.CompilerParams(vmem_limit_bytes=48 << 20),
    )(scalars, mine, other, rhs, early, *[near[p] for p, _ in pairs], *[far[p] for p, _ in pairs])


def local(rhs, factor, inverses):
    x, y, z = (lax.axis_index(a) for a in ("x", "y", "z"))
    core = lax.axis_index("rhs")
    place = (y * 4 + z) * 4 + x
    owner = place < 4
    zero = jnp.zeros((), BF)

    slabs = loads(rhs, factor[0].reshape(1, 512, 1024))
    outward = {
        (p, d): permute(slabs[4 * p + d], [((i, 0, 0), (i, 0, d) if p else (i, d, 0)) for i in range(4)])
        for p, d in ((0, 3), (0, 1), (1, 1), (0, 2), (1, 2), (1, 3))
    }
    hold_a = jnp.where(owner, slabs[0], zero) + outward[0, 1] + outward[0, 2] + outward[0, 3]
    own_b, hold_a = lax.optimization_barrier((slabs[4], hold_a))
    hold_b = jnp.where(owner, own_b, zero) + outward[1, 1] + outward[1, 2] + outward[1, 3]

    def finish(hold, axis):
        tail = [hold[512:, k * 128:(k + 1) * 128] for k in range(4)]
        message = lambda d: jnp.concatenate([hold[:512, d * 128:(d + 1) * 128]] + tail, axis=0)
        mine = jnp.where((z if axis == "y" else y) == 0, message(0), zero)
        for d in (1, 3, 2):
            if axis == "y":
                moves = [((i, j, 0), (i, j, d)) for i in range(4) for j in range(4)]
            else:
                moves = [((i, 0, j), (i, d, j)) for i in range(4) for j in range(4)]
            mine = mine + permute(message(d), moves)
        return mine

    mine_a = finish(hold_a, "y")
    mine_b = finish(hold_b, "z")

    inverse = lax.dynamic_index_in_dim(inverses, x, 0, keepdims=False)
    rounded = lax.reduce_precision(inverse, 8, 7)
    inverse = (rounded.astype(BF), (inverse - rounded).astype(BF))
    where = jnp.stack([core, x, y, z]).astype(jnp.int32)
    state = mine_a[:512].astype(F32) + mine_b[:512].astype(F32)
    state, *inverse = lax.optimization_barrier((state, *inverse))
    sent_0, = step(where, state, inverse)
    gots = [hop(sent_0, (0, 1)), hop(sent_0, (0, 3)), hop(sent_0, (0, 2))]

    piece_a, piece_b, _ = lax.optimization_barrier((mine_a[512:], mine_b[512:], sent_0))
    near_a, near_b = swap(piece_a, "y", 1), swap(piece_b, "z", 1)
    near_a, near_b, *gots = lax.optimization_barrier((near_a, near_b, *gots))

    def complete(piece, near, axis):
        two = jnp.stack([piece, near])
        return jnp.concatenate([two, swap(two, axis, 3)], axis=0).reshape(4, 3, 128, 128)

    top, bottom = complete(piece_a, near_a, "y"), complete(piece_b, near_b, "z")
    block = (top, bottom, lax.ppermute(top, "rhs", [(0, 1), (1, 0)]), lax.ppermute(bottom, "rhs", [(0, 1), (1, 0)]))

    panel_0 = jnp.where(x == 0, sent_0, gots[0] + gots[1] + gots[2])
    early_0 = lax.all_gather(panel_0, ("y", "z"), axis=0)
    state, sent_1 = step(where, state, inverse, block, 0, gots)
    gots_1 = [hop(sent_1, (1, 2)), hop(sent_1, (1, 3))]
    state, sent_2 = step(where, state, inverse, block, 1, gots_1)
    got = hop(sent_2, (2, 3))
    state, sent = step(where, state, inverse, block, 2, (got,))
    sent_2 = jnp.where(x == 2, sent_2, sent_1)
    sent = jnp.where(x == 3, sent, sent_2)
    back = hop(sent, (1, 0), (2, 1), (3, 2))
    far = hop(sent, (2, 0), (3, 1))
    wrap = hop(sent, (3, 0))
    panel_1 = jnp.where(x == 1, sent, jnp.where(x == 0, back, gots_1[0] + gots_1[1]))
    panel_2 = jnp.where(x == 2, sent, jnp.where(x == 3, got, jnp.where(x == 1, back, far)))
    panel_3 = jnp.where(x == 3, sent, jnp.where(x == 2, back, jnp.where(x == 1, far, wrap)))
    cat = lambda *v: jnp.concatenate(v, axis=0)
    parts = [panel_1[:384], cat(panel_1[384:], panel_2[:256]), cat(panel_2[256:], panel_3[:128]), panel_3[128:]]
    near, flat_factor, early_0, far_late = spread(parts, factor.reshape(2, 512, 1024), early_0)
    other_factor = lax.ppermute(flat_factor, "rhs", [(0, 1), (1, 0)])

    scalars = jnp.concatenate([places(y, z), jnp.stack([place, core])]).astype(jnp.int32)
    return update(scalars, flat_factor, other_factor, rhs, early_0, near, far_late)


def solution(mesh):
    grid = Mesh(mesh.devices.reshape(4, 4, 4, 2), ("y", "z", "x", "rhs"))
    return jax.shard_map(
        local,
        mesh=grid,
        in_specs=(P(None, ROWS, "rhs"), P(None, ROWS, None, "rhs"), P()),
        out_specs=P(None, ROWS, "rhs"),
        check_vma=False,
    )
```

```python
import jax
import jax.numpy as jnp
from jax import lax
from jax.experimental import pallas as pl
from jax.experimental.pallas import tpu as pltpu
from jax.sharding import Mesh, PartitionSpec as P

ROWS = ("y", "z", "x")
BF = jnp.bfloat16
F32 = jnp.float32
ALL = [(j, k) for j in range(4) for k in range(4)]
ORDERS = (
    (("y", 1), ("y", 3), ("z", 1), ("z", 3)),
    (("y", 3), ("y", 1), ("z", 3), ("z", 1)),
    (("z", 1), ("z", 3), ("y", 1), ("y", 3)),
    (("z", 3), ("z", 1), ("y", 3), ("y", 1)),
)


def flat(x, y, z):
    return ((y % 4) * 4 + (z % 4)) * 4 + (x % 4)


def permute(value, moves):
    return lax.ppermute(value, ROWS, [(flat(*a), flat(*b)) for a, b in moves])


def hop(value, *planes):
    return permute(value, [((a, j, k), (b, j, k)) for a, b in planes for j, k in ALL])


def swap(value, axis, flip):
    return lax.ppermute(value, axis, [(i, i ^ flip) for i in range(4)])


def spread(parts, early, other):
    parts = [p[None] for p in parts]
    for step in range(3):
        got = [swap(p, *order[step]) for p, order in zip(parts, ORDERS)]
        if step == 0:
            early, got[3] = lax.optimization_barrier((early, got[3]))
        parts = [jnp.concatenate([p, g], axis=0) for p, g in zip(parts, got)]
    got = [swap(p, *order[3]) for p, order in zip(parts, ORDERS)]
    other, *got = lax.optimization_barrier((other, *got))
    return parts, early, other, got


def places(y, z):
    sites = jnp.arange(16, dtype=jnp.int32)
    tables = []
    for order in ORDERS:
        off = {"y": (sites // 4) ^ y, "z": (sites % 4) ^ z}
        total = jnp.zeros_like(sites)
        for step, (axis, flip) in enumerate(order):
            o = off[axis]
            upper = o >> 1
            bit = upper if flip == 3 else (o & 1) ^ upper
            total = total + (bit << step)
        tables.append(total)
    return jnp.stack(tables).reshape(-1)


def split(value):
    high = value.astype(BF)
    return high, (value - high.astype(F32)).astype(BF)


def put_piece(factor_ref, base, out_ref):
    for u in range(12):
        rows = slice(base + u % 2 * 32, base + u % 2 * 32 + 32)
        at = 512 + u % 3 * 32
        out_ref[at:at + 32, u // 3 * 128:(u // 3 + 1) * 128] = factor_ref[0, rows, u // 2 * 128:(u // 2 + 1) * 128]


def load_kernel(rhs_ref, factor_ref, *outs):
    for d in range(4):
        for j in range(4):
            lanes = slice(j * 128, (j + 1) * 128)
            at = d * 512 + j * 128
            outs[d][:512, lanes] = rhs_ref[0, :, at:at + 128].astype(BF)
            at = j * 512 + d * 128
            outs[4 + d][:512, lanes] = split(rhs_ref[0, :, at:at + 128])[1]
        put_piece(factor_ref, d * 64, outs[d])
        put_piece(factor_ref, 256 + d * 64, outs[4 + d])


def loads(rhs, factor):
    return pl.pallas_call(
        load_kernel,
        grid=(1,),
        in_specs=[pl.BlockSpec((1, 512, 2048), lambda i: (0, 0, 0)), pl.BlockSpec((1, 512, 1024), lambda i: (0, 0, 0))],
        out_specs=[pl.BlockSpec((608, 512), lambda i: (0, 0))] * 8,
        out_shape=[jax.ShapeDtypeStruct((608, 512), BF)] * 8,
        compiler_params=pltpu.CompilerParams(vmem_limit_bytes=48 << 20),
    )(rhs, factor)


def solve(high_ref, low_ref, state):
    high, low = split(state)
    dot = lambda a, b: jnp.dot(a, b, preferred_element_type=F32)
    return (dot(high_ref[...], high) + dot(high_ref[...], low) + dot(low_ref[...], high)).astype(BF)


def first_kernel(scalars, state_ref, high_ref, low_ref, sent_ref):
    sent_ref[...] = solve(high_ref, low_ref, state_ref[...])


def step_kernel(panel, scalars, state_ref, high_ref, low_ref, *refs):
    dot = lambda a, b: jnp.dot(a, b, preferred_element_type=F32)
    pieces, refs, block_ref = refs[:4], refs[4:-1], refs[-1]
    core = scalars[0]
    for source in range(2):
        half = core if source == 0 else 1 - core
        for side in range(2):
            for i in range(4):
                off = scalars[2 + side] ^ i
                at = off ^ (off >> 1)
                rows = slice(side * 256 + i * 64, side * 256 + i * 64 + 64)
                for h in range(2):
                    block_ref[half, rows, h * 128:(h + 1) * 128] = pieces[2 * source + side][at, 0, h * 64:(h + 1) * 64]
    gots = refs[:3 - panel]
    got = sum(g[...] for g in gots)
    state = state_ref[...] - dot(block_ref[0], got[:256]) - dot(block_ref[1], got[256:])
    next_ref, new_ref = refs[3 - panel:]
    next_ref[...] = state
    new_ref[...] = solve(high_ref, low_ref, state)


def step(scalars, state, inverse, factor=None, panel=None, more=()):
    full = lambda shape: pl.BlockSpec(shape, lambda i, s: (0, 0))
    part = pl.BlockSpec((4, 1, 128, 128), lambda i, s: (0, panel, 0, 0))
    tall, square = full((512, 128)), full((512, 512))
    shapes = [jax.ShapeDtypeStruct((512, 128), BF)]
    scratch = []
    if panel is None:
        kernel, ins, factor = first_kernel, [], ()
    else:
        kernel, ins = lambda *refs: step_kernel(panel, *refs), [part] * 4 + [tall] * len(more)
        scratch = [pltpu.VMEM((2, 512, 256), BF)]
        shapes = [jax.ShapeDtypeStruct((512, 128), F32)] + shapes
    return pl.pallas_call(
        kernel,
        grid_spec=pltpu.PrefetchScalarGridSpec(
            num_scalar_prefetch=1,
            grid=(1,),
            in_specs=[tall, square, square] + ins,
            out_specs=[full(v.shape) for v in shapes],
            scratch_shapes=scratch,
        ),
        out_shape=shapes,
        compiler_params=pltpu.CompilerParams(vmem_limit_bytes=32 << 20),
    )(scalars, state, *inverse, *factor, *more)


def update_kernel(scalars, mine_ref, other_ref, rhs_ref, early_ref, *rest):
    near, far, out_ref, sent_ref = rest[:8], rest[8:16], rest[16], rest[17]
    j = pl.program_id(0)
    place, core = scalars[64], scalars[65]

    def rows(panel, half, size=256):
        return pl.ds(pl.multiple_of((core ^ (half // 256)) * 1024 + panel * 256 + half % 256, 128), size)

    def put(part_ref, p, lanes):
        for u in range(3):
            row = 512 + p * 384 + u * 128
            sent_ref[rows(row // 512, row % 512, 128), lanes] = part_ref[0, u * 128:(u + 1) * 128]

    for h in range(2):
        lanes = slice(h * 128, (h + 1) * 128)
        for half in (0, 256):
            sent_ref[rows(0, half), lanes] = early_ref[h, half:half + 256]
        for p in range(4):
            low = scalars[p * 16 + 2 * j + h] < 8

            @pl.when(low)
            def _():
                put(near[p * 2 + h], p, lanes)

            @pl.when(jnp.logical_not(low))
            def _():
                put(far[p * 2 + h], p, lanes)
    dot = lambda a, b: jnp.dot(a, b, preferred_element_type=F32)
    for c in range(2):
        out_ref[c] = rhs_ref[c] - (dot(mine_ref[c], sent_ref[:1024]) + dot(other_ref[c], sent_ref[1024:]))

    @pl.when(place < 4)
    def _():
        for half in (0, 256):
            out_ref[0, half:half + 256] = sent_ref[rows(place, half), :].astype(F32)


def update(scalars, mine, other, rhs, early, near, far):
    cycles, tile, depth = mine.shape
    pairs = [(p, h) for p in range(4) for h in range(2)]
    near_specs = [
        pl.BlockSpec((1, 384, 128), lambda j, s, p=p, h=h: (jnp.minimum(s[p * 16 + 2 * j + h], 7), 0, 0))
        for p, h in pairs
    ]
    far_specs = [
        pl.BlockSpec((1, 384, 128), lambda j, s, p=p, h=h: (jnp.maximum(s[p * 16 + 2 * j + h] - 8, 0), 0, 0))
        for p, h in pairs
    ]
    return pl.pallas_call(
        update_kernel,
        grid_spec=pltpu.PrefetchScalarGridSpec(
            num_scalar_prefetch=1,
            grid=(rhs.shape[2] // 256,),
            in_specs=[
                pl.BlockSpec((cycles, tile, depth), lambda j, s: (0, 0, 0)),
                pl.BlockSpec((cycles, tile, depth), lambda j, s: (0, 0, 0)),
                pl.BlockSpec((cycles, tile, 256), lambda j, s: (0, 0, j)),
                pl.BlockSpec((2, 512, 128), lambda j, s: (j, 0, 0)),
            ] + near_specs + far_specs,
            out_specs=pl.BlockSpec((cycles, tile, 256), lambda j, s: (0, 0, j)),
            scratch_shapes=[pltpu.VMEM((2048, 256), BF)],
        ),
        out_shape=jax.ShapeDtypeStruct(rhs.shape, F32),
        compiler_params=pltpu.CompilerParams(vmem_limit_bytes=48 << 20),
    )(scalars, mine, other, rhs, early, *[near[p] for p, _ in pairs], *[far[p] for p, _ in pairs])


def local(rhs, factor, inverses):
    x, y, z = (lax.axis_index(a) for a in ("x", "y", "z"))
    core = lax.axis_index("rhs")
    place = (y * 4 + z) * 4 + x
    owner = place < 4
    zero = jnp.zeros((), BF)

    slabs = loads(rhs, factor[0].reshape(1, 512, 1024))
    outward = {
        (p, d): permute(slabs[4 * p + d], [((i, 0, 0), (i, 0, d) if p else (i, d, 0)) for i in range(4)])
        for p, d in ((0, 3), (0, 1), (1, 1), (0, 2), (1, 2), (1, 3))
    }
    hold_a = jnp.where(owner, slabs[0], zero) + outward[0, 1] + outward[0, 2] + outward[0, 3]
    own_b, hold_a = lax.optimization_barrier((slabs[4], hold_a))
    hold_b = jnp.where(owner, own_b, zero) + outward[1, 1] + outward[1, 2] + outward[1, 3]

    def finish(hold, axis):
        tail = [hold[512:, k * 128:(k + 1) * 128] for k in range(4)]
        message = lambda d: jnp.concatenate([hold[:512, d * 128:(d + 1) * 128]] + tail, axis=0)
        mine = jnp.where((z if axis == "y" else y) == 0, message(0), zero)
        for d in (1, 3, 2):
            if axis == "y":
                moves = [((i, j, 0), (i, j, d)) for i in range(4) for j in range(4)]
            else:
                moves = [((i, 0, j), (i, d, j)) for i in range(4) for j in range(4)]
            mine = mine + permute(message(d), moves)
        return mine

    mine_a = finish(hold_a, "y")
    mine_b = finish(hold_b, "z")

    inverse = lax.dynamic_index_in_dim(inverses, x, 0, keepdims=False)
    rounded = lax.reduce_precision(inverse, 8, 7)
    inverse = (rounded.astype(BF), (inverse - rounded).astype(BF))
    where = jnp.stack([core, x, y, z]).astype(jnp.int32)
    state = mine_a[:512].astype(F32) + mine_b[:512].astype(F32)
    state, *inverse = lax.optimization_barrier((state, *inverse))
    sent_0, = step(where, state, inverse)
    gots = [hop(sent_0, (0, 1)), hop(sent_0, (0, 3)), hop(sent_0, (0, 2))]

    piece_a, piece_b, _ = lax.optimization_barrier((mine_a[512:], mine_b[512:], sent_0))
    near_a, near_b = swap(piece_a, "y", 1), swap(piece_b, "z", 1)
    near_a, near_b, *gots = lax.optimization_barrier((near_a, near_b, *gots))

    def complete(piece, near, axis):
        two = jnp.stack([piece, near])
        return jnp.concatenate([two, swap(two, axis, 3)], axis=0).reshape(4, 3, 128, 128)

    top, bottom = complete(piece_a, near_a, "y"), complete(piece_b, near_b, "z")
    block = (top, bottom, lax.ppermute(top, "rhs", [(0, 1), (1, 0)]), lax.ppermute(bottom, "rhs", [(0, 1), (1, 0)]))

    panel_0 = jnp.where(x == 0, sent_0, gots[0] + gots[1] + gots[2])
    early_0 = lax.all_gather(panel_0, ("y", "z"), axis=0)
    state, sent_1 = step(where, state, inverse, block, 0, gots)
    gots_1 = [hop(sent_1, (1, 2)), hop(sent_1, (1, 3))]
    state, sent_2 = step(where, state, inverse, block, 1, gots_1)
    got = hop(sent_2, (2, 3))
    state, sent = step(where, state, inverse, block, 2, (got,))
    sent_2 = jnp.where(x == 2, sent_2, sent_1)
    sent = jnp.where(x == 3, sent, sent_2)
    back = hop(sent, (1, 0), (2, 1), (3, 2))
    far = hop(sent, (2, 0), (3, 1))
    wrap = hop(sent, (3, 0))
    panel_1 = jnp.where(x == 1, sent, jnp.where(x == 0, back, gots_1[0] + gots_1[1]))
    panel_2 = jnp.where(x == 2, sent, jnp.where(x == 3, got, jnp.where(x == 1, back, far)))
    panel_3 = jnp.where(x == 3, sent, jnp.where(x == 2, back, jnp.where(x == 1, far, wrap)))
    cat = lambda *v: jnp.concatenate(v, axis=0)
    parts = [panel_1[:384], cat(panel_1[384:], panel_2[:256]), cat(panel_2[256:], panel_3[:128]), panel_3[128:]]
    flat_factor = factor.reshape(2, 512, 1024)
    other_factor = lax.ppermute(flat_factor, "rhs", [(0, 1), (1, 0)])
    near, early_0, other_factor, far_late = spread(parts, early_0, other_factor)
    scalars = jnp.concatenate([places(y, z), jnp.stack([place, core])]).astype(jnp.int32)
    return update(scalars, flat_factor, other_factor, rhs, early_0, near, far_late)


def solution(mesh):
    grid = Mesh(mesh.devices.reshape(4, 4, 4, 2), ("y", "z", "x", "rhs"))
    return jax.shard_map(
        local,
        mesh=grid,
        in_specs=(P(None, ROWS, "rhs"), P(None, ROWS, None, "rhs"), P()),
        out_specs=P(None, ROWS, "rhs"),
        check_vma=False,
    )
```

```python
import jax
import jax.numpy as jnp
from jax import lax
from jax.experimental import pallas as pl
from jax.experimental.pallas import tpu as pltpu
from jax.sharding import Mesh, PartitionSpec as P

ROWS = ("y", "z", "x")
BF = jnp.bfloat16
F32 = jnp.float32
ALL = [(j, k) for j in range(4) for k in range(4)]
ORDERS = (
    (("y", 1), ("y", 3), ("z", 1), ("z", 3)),
    (("y", 3), ("y", 1), ("z", 3), ("z", 1)),
    (("z", 1), ("z", 3), ("y", 1), ("y", 3)),
    (("z", 3), ("z", 1), ("y", 3), ("y", 1)),
)


def flat(x, y, z):
    return ((y % 4) * 4 + (z % 4)) * 4 + (x % 4)


def permute(value, moves):
    return lax.ppermute(value, ROWS, [(flat(*a), flat(*b)) for a, b in moves])


def hop(value, *planes):
    return permute(value, [((a, j, k), (b, j, k)) for a, b in planes for j, k in ALL])


def swap(value, axis, flip):
    return lax.ppermute(value, axis, [(i, i ^ flip) for i in range(lax.axis_size(axis))])


def spread(parts, early, other):
    parts = [p[None] for p in parts]
    for step in range(3):
        got = [swap(p, *order[step]) for p, order in zip(parts, ORDERS)]
        if step == 1:
            early, got[3] = lax.optimization_barrier((early, got[3]))
        parts = [jnp.concatenate([p, g], axis=0) for p, g in zip(parts, got)]
    got = [swap(p, *order[3]) for p, order in zip(parts, ORDERS)]
    other, *got = lax.optimization_barrier((other, *got))
    return parts, early, other, got


def places(y, z):
    sites = jnp.arange(16, dtype=jnp.int32)
    tables = []
    for order in ORDERS:
        off = {"y": (sites // 4) ^ y, "z": (sites % 4) ^ z}
        total = jnp.zeros_like(sites)
        for step, (axis, flip) in enumerate(order):
            o = off[axis]
            upper = o >> 1
            bit = upper if flip == 3 else (o & 1) ^ upper
            total = total + (bit << step)
        tables.append(total)
    return jnp.stack(tables).reshape(-1)


def split(value):
    high = value.astype(BF)
    return high, (value - high.astype(F32)).astype(BF)


def put_piece(factor_ref, base, out_ref):
    for u in range(12):
        rows = slice(base + u % 2 * 32, base + u % 2 * 32 + 32)
        at = 512 + u % 3 * 32
        out_ref[at:at + 32, u // 3 * 128:(u // 3 + 1) * 128] = factor_ref[0, rows, u // 2 * 128:(u // 2 + 1) * 128]


def load_kernel(rhs_ref, factor_ref, *outs):
    for d in range(4):
        for j in range(4):
            lanes = slice(j * 128, (j + 1) * 128)
            at = d * 512 + j * 128
            outs[d][:512, lanes] = rhs_ref[0, :, at:at + 128].astype(BF)
            at = j * 512 + d * 128
            outs[4 + d][:512, lanes] = split(rhs_ref[0, :, at:at + 128])[1]
        put_piece(factor_ref, d * 64, outs[d])
        put_piece(factor_ref, 256 + d * 64, outs[4 + d])


def loads(rhs, factor):
    return pl.pallas_call(
        load_kernel,
        grid=(1,),
        in_specs=[pl.BlockSpec((1, 512, 2048), lambda i: (0, 0, 0)), pl.BlockSpec((1, 512, 1024), lambda i: (0, 0, 0))],
        out_specs=[pl.BlockSpec((608, 512), lambda i: (0, 0))] * 8,
        out_shape=[jax.ShapeDtypeStruct((608, 512), BF)] * 8,
        compiler_params=pltpu.CompilerParams(vmem_limit_bytes=48 << 20),
    )(rhs, factor)


def solve(high_ref, low_ref, state):
    high, low = split(state)
    dot = lambda a, b: jnp.dot(a, b, preferred_element_type=F32)
    return (dot(high_ref[...], high) + dot(high_ref[...], low) + dot(low_ref[...], high)).astype(BF)


def first_kernel(scalars, state_ref, high_ref, low_ref, sent_ref):
    sent_ref[...] = solve(high_ref, low_ref, state_ref[...])


def step_kernel(panel, scalars, state_ref, high_ref, low_ref, *refs):
    dot = lambda a, b: jnp.dot(a, b, preferred_element_type=F32)
    pieces, refs, block_ref = refs[:4], refs[4:-1], refs[-1]
    core = scalars[0]
    for source in range(2):
        half = core if source == 0 else 1 - core
        for side in range(2):
            for i in range(4):
                off = scalars[2 + side] ^ i
                at = off ^ (off >> 1)
                rows = slice(side * 256 + i * 64, side * 256 + i * 64 + 64)
                for h in range(2):
                    block_ref[half, rows, h * 128:(h + 1) * 128] = pieces[2 * source + side][at, 0, h * 64:(h + 1) * 64]
    gots = refs[:3 - panel]
    got = sum(g[...] for g in gots)
    state = state_ref[...] - dot(block_ref[0], got[:256]) - dot(block_ref[1], got[256:])
    next_ref, new_ref = refs[3 - panel:]
    next_ref[...] = state
    new_ref[...] = solve(high_ref, low_ref, state)


def step(scalars, state, inverse, factor=None, panel=None, more=()):
    full = lambda shape: pl.BlockSpec(shape, lambda i, s: (0, 0))
    part = pl.BlockSpec((4, 1, 128, 128), lambda i, s: (0, panel, 0, 0))
    tall, square = full((512, 128)), full((512, 512))
    shapes = [jax.ShapeDtypeStruct((512, 128), BF)]
    scratch = []
    if panel is None:
        kernel, ins, factor = first_kernel, [], ()
    else:
        kernel, ins = lambda *refs: step_kernel(panel, *refs), [part] * 4 + [tall] * len(more)
        scratch = [pltpu.VMEM((2, 512, 256), BF)]
        shapes = [jax.ShapeDtypeStruct((512, 128), F32)] + shapes
    return pl.pallas_call(
        kernel,
        grid_spec=pltpu.PrefetchScalarGridSpec(
            num_scalar_prefetch=1,
            grid=(1,),
            in_specs=[tall, square, square] + ins,
            out_specs=[full(v.shape) for v in shapes],
            scratch_shapes=scratch,
        ),
        out_shape=shapes,
        compiler_params=pltpu.CompilerParams(vmem_limit_bytes=32 << 20),
    )(scalars, state, *inverse, *factor, *more)


def update_kernel(scalars, mine_ref, other_ref, rhs_ref, early_ref, *rest):
    near, far, out_ref, sent_ref = rest[:8], rest[8:16], rest[16], rest[17]
    j = pl.program_id(0)
    place, core = scalars[64], scalars[65]

    def rows(panel, half, size=256):
        return pl.ds(pl.multiple_of((core ^ (half // 256)) * 1024 + panel * 256 + half % 256, 128), size)

    def put(part_ref, p, lanes):
        for u in range(3):
            row = 512 + p * 384 + u * 128
            sent_ref[rows(row // 512, row % 512, 128), lanes] = part_ref[0, u * 128:(u + 1) * 128]

    for h in range(2):
        lanes = slice(h * 128, (h + 1) * 128)
        for half in (0, 256):
            sent_ref[rows(0, half), lanes] = early_ref[h, half:half + 256]
        for p in range(4):
            low = scalars[p * 16 + 2 * j + h] < 8

            @pl.when(low)
            def _():
                put(near[p * 2 + h], p, lanes)

            @pl.when(jnp.logical_not(low))
            def _():
                put(far[p * 2 + h], p, lanes)
    dot = lambda a, b: jnp.dot(a, b, preferred_element_type=F32)
    for c in range(2):
        out_ref[c] = rhs_ref[c] - (dot(mine_ref[c], sent_ref[:1024]) + dot(other_ref[c], sent_ref[1024:]))

    @pl.when(place < 4)
    def _():
        for half in (0, 256):
            out_ref[0, half:half + 256] = sent_ref[rows(place, half), :].astype(F32)


def update(scalars, mine, other, rhs, early, near, far):
    cycles, tile, depth = mine.shape
    pairs = [(p, h) for p in range(4) for h in range(2)]
    near_specs = [
        pl.BlockSpec((1, 384, 128), lambda j, s, p=p, h=h: (jnp.minimum(s[p * 16 + 2 * j + h], 7), 0, 0))
        for p, h in pairs
    ]
    far_specs = [
        pl.BlockSpec((1, 384, 128), lambda j, s, p=p, h=h: (jnp.maximum(s[p * 16 + 2 * j + h] - 8, 0), 0, 0))
        for p, h in pairs
    ]
    return pl.pallas_call(
        update_kernel,
        grid_spec=pltpu.PrefetchScalarGridSpec(
            num_scalar_prefetch=1,
            grid=(rhs.shape[2] // 256,),
            in_specs=[
                pl.BlockSpec((cycles, tile, depth), lambda j, s: (0, 0, 0)),
                pl.BlockSpec((cycles, tile, depth), lambda j, s: (0, 0, 0)),
                pl.BlockSpec((cycles, tile, 256), lambda j, s: (0, 0, j)),
                pl.BlockSpec((2, 512, 128), lambda j, s: (j, 0, 0)),
            ] + near_specs + far_specs,
            out_specs=pl.BlockSpec((cycles, tile, 256), lambda j, s: (0, 0, j)),
            scratch_shapes=[pltpu.VMEM((2048, 256), BF)],
        ),
        out_shape=jax.ShapeDtypeStruct(rhs.shape, F32),
        compiler_params=pltpu.CompilerParams(vmem_limit_bytes=48 << 20),
    )(scalars, mine, other, rhs, early, *[near[p] for p, _ in pairs], *[far[p] for p, _ in pairs])


def local(rhs, factor, inverses):
    x, y, z = (lax.axis_index(a) for a in ("x", "y", "z"))
    core = lax.axis_index("rhs")
    place = (y * 4 + z) * 4 + x
    owner = place < 4
    zero = jnp.zeros((), BF)

    slabs = loads(rhs, factor[0].reshape(1, 512, 1024))
    outward = {
        (p, d): permute(slabs[4 * p + d], [((i, 0, 0), (i, 0, d) if p else (i, d, 0)) for i in range(4)])
        for p, d in ((0, 3), (0, 1), (1, 1), (0, 2), (1, 2), (1, 3))
    }
    hold_a = jnp.where(owner, slabs[0], zero) + outward[0, 1] + outward[0, 2] + outward[0, 3]
    own_b, hold_a = lax.optimization_barrier((slabs[4], hold_a))
    hold_b = jnp.where(owner, own_b, zero) + outward[1, 1] + outward[1, 2] + outward[1, 3]

    def finish(hold, axis):
        tail = [hold[512:, k * 128:(k + 1) * 128] for k in range(4)]
        message = lambda d: jnp.concatenate([hold[:512, d * 128:(d + 1) * 128]] + tail, axis=0)
        mine = jnp.where((z if axis == "y" else y) == 0, message(0), zero)
        for d in (1, 3, 2):
            if axis == "y":
                moves = [((i, j, 0), (i, j, d)) for i in range(4) for j in range(4)]
            else:
                moves = [((i, 0, j), (i, d, j)) for i in range(4) for j in range(4)]
            mine = mine + permute(message(d), moves)
        return mine

    mine_a = finish(hold_a, "y")
    mine_b = finish(hold_b, "z")

    inverse = lax.dynamic_index_in_dim(inverses, x, 0, keepdims=False)
    rounded = lax.reduce_precision(inverse, 8, 7)
    inverse = (rounded.astype(BF), (inverse - rounded).astype(BF))
    where = jnp.stack([core, x, y, z]).astype(jnp.int32)
    state = mine_a[:512].astype(F32) + mine_b[:512].astype(F32)
    piece_a, piece_b = mine_a[512:], mine_b[512:]
    state, *inverse = lax.optimization_barrier((state, *inverse))
    sent_0, = step(where, state, inverse)
    gots = [hop(sent_0, (0, 1)), hop(sent_0, (0, 3)), hop(sent_0, (0, 2))]

    two_a = jnp.stack([piece_a, swap(piece_a, "y", 1)])
    two_b = jnp.stack([piece_b, swap(piece_b, "z", 1)])
    two_a, two_b, _ = lax.optimization_barrier((two_a, two_b, sent_0))
    four_a, four_b, *gots = lax.optimization_barrier((swap(two_a, "y", 3), swap(two_b, "z", 3), *gots))
    top = jnp.concatenate([two_a, four_a], axis=0).reshape(4, 3, 128, 128)
    bottom = jnp.concatenate([two_b, four_b], axis=0).reshape(4, 3, 128, 128)
    block = (top, bottom, swap(top, "rhs", 1), swap(bottom, "rhs", 1))

    panel_0 = jnp.where(x == 0, sent_0, gots[0] + gots[1] + gots[2])
    early_0 = lax.all_gather(panel_0, ("y", "z"), axis=0)
    state, sent_1 = step(where, state, inverse, block, 0, gots)
    gots_1 = [hop(sent_1, (1, 2)), hop(sent_1, (1, 3))]
    state, sent_2 = step(where, state, inverse, block, 1, gots_1)
    got = hop(sent_2, (2, 3))
    state, sent = step(where, state, inverse, block, 2, (got,))
    sent_2 = jnp.where(x == 2, sent_2, sent_1)
    sent = jnp.where(x == 3, sent, sent_2)
    back = hop(sent, (1, 0), (2, 1), (3, 2))
    far = hop(sent, (2, 0), (3, 1))
    wrap = hop(sent, (3, 0))
    panel_1 = jnp.where(x == 1, sent, jnp.where(x == 0, back, gots_1[0] + gots_1[1]))
    panel_2 = jnp.where(x == 2, sent, jnp.where(x == 3, got, jnp.where(x == 1, back, far)))
    panel_3 = jnp.where(x == 3, sent, jnp.where(x == 2, back, jnp.where(x == 1, far, wrap)))
    cat = lambda *v: jnp.concatenate(v, axis=0)
    parts = [panel_1[:384], cat(panel_1[384:], panel_2[:256]), cat(panel_2[256:], panel_3[:128]), panel_3[128:]]
    flat_factor = factor.reshape(2, 512, 1024)
    other_factor = lax.ppermute(flat_factor, "rhs", [(0, 1), (1, 0)])
    near, early_0, other_factor, far_late = spread(parts, early_0, other_factor)
    scalars = jnp.concatenate([places(y, z), jnp.stack([place, core])]).astype(jnp.int32)
    return update(scalars, flat_factor, other_factor, rhs, early_0, near, far_late)


def solution(mesh):
    grid = Mesh(mesh.devices.reshape(4, 4, 4, 2), ("y", "z", "x", "rhs"))
    return jax.shard_map(
        local,
        mesh=grid,
        in_specs=(P(None, ROWS, "rhs"), P(None, ROWS, None, "rhs"), P()),
        out_specs=P(None, ROWS, "rhs"),
        check_vma=False,
    )
```

```python
import jax
import jax.numpy as jnp
from jax import lax
from jax.experimental import pallas as pl
from jax.experimental.pallas import tpu as pltpu
from jax.sharding import Mesh, PartitionSpec as P

ROWS = ("y", "z", "x")
BF = jnp.bfloat16
F32 = jnp.float32
ALL = [(j, k) for j in range(4) for k in range(4)]
ORDERS = (
    (("y", 1), ("y", 3), ("z", 1), ("z", 3)),
    (("y", 3), ("y", 1), ("z", 3), ("z", 1)),
    (("z", 1), ("z", 3), ("y", 1), ("y", 3)),
    (("z", 3), ("z", 1), ("y", 3), ("y", 1)),
)


def flat(x, y, z):
    return ((y % 4) * 4 + (z % 4)) * 4 + (x % 4)


def permute(value, moves):
    return lax.ppermute(value, ROWS, [(flat(*a), flat(*b)) for a, b in moves])


def hop(value, *planes):
    return permute(value, [((a, j, k), (b, j, k)) for a, b in planes for j, k in ALL])


def swap(value, axis, flip):
    return lax.ppermute(value, axis, [(i, i ^ flip) for i in range(4)])


def spread(parts, early, other):
    parts = [p[None] for p in parts]
    for step in range(3):
        got = [swap(p, *order[step]) for p, order in zip(parts, ORDERS)]
        if step == 1:
            early, got[3] = lax.optimization_barrier((early, got[3]))
        parts = [jnp.concatenate([p, g], axis=0) for p, g in zip(parts, got)]
    got = [swap(p, *order[3]) for p, order in zip(parts, ORDERS)]
    other, *got = lax.optimization_barrier((other, *got))
    return parts, early, other, got


def places(y, z):
    sites = jnp.arange(16, dtype=jnp.int32)
    tables = []
    for order in ORDERS:
        off = {"y": (sites // 4) ^ y, "z": (sites % 4) ^ z}
        total = jnp.zeros_like(sites)
        for step, (axis, flip) in enumerate(order):
            o = off[axis]
            upper = o >> 1
            bit = upper if flip == 3 else (o & 1) ^ upper
            total = total + (bit << step)
        tables.append(total)
    return jnp.stack(tables).reshape(-1)


def split(value):
    high = value.astype(BF)
    return high, (value - high.astype(F32)).astype(BF)


def put_piece(factor_ref, base, out_ref):
    for u in range(12):
        rows = slice(base + u % 2 * 32, base + u % 2 * 32 + 32)
        at = 512 + u % 3 * 32
        out_ref[at:at + 32, u // 3 * 128:(u // 3 + 1) * 128] = factor_ref[0, rows, u // 2 * 128:(u // 2 + 1) * 128]


def load_kernel(rhs_ref, factor_ref, *outs):
    for d in range(4):
        for j in range(4):
            lanes = slice(j * 128, (j + 1) * 128)
            at = d * 512 + j * 128
            outs[d][:512, lanes] = rhs_ref[0, :, at:at + 128].astype(BF)
            at = j * 512 + d * 128
            outs[4 + d][:512, lanes] = split(rhs_ref[0, :, at:at + 128])[1]
        put_piece(factor_ref, d * 64, outs[d])
        put_piece(factor_ref, 256 + d * 64, outs[4 + d])


def loads(rhs, factor):
    return pl.pallas_call(
        load_kernel,
        grid=(1,),
        in_specs=[pl.BlockSpec((1, 512, 2048), lambda i: (0, 0, 0)), pl.BlockSpec((1, 512, 1024), lambda i: (0, 0, 0))],
        out_specs=[pl.BlockSpec((608, 512), lambda i: (0, 0))] * 8,
        out_shape=[jax.ShapeDtypeStruct((608, 512), BF)] * 8,
        compiler_params=pltpu.CompilerParams(vmem_limit_bytes=48 << 20),
    )(rhs, factor)


def solve(high_ref, low_ref, state):
    high, low = split(state)
    dot = lambda a, b: jnp.dot(a, b, preferred_element_type=F32)
    return (dot(high_ref[...], high) + dot(high_ref[...], low) + dot(low_ref[...], high)).astype(BF)


def first_kernel(scalars, state_ref, high_ref, low_ref, sent_ref):
    sent_ref[...] = solve(high_ref, low_ref, state_ref[...])


def step_kernel(panel, scalars, state_ref, high_ref, low_ref, *refs):
    dot = lambda a, b: jnp.dot(a, b, preferred_element_type=F32)
    pieces, refs, block_ref = refs[:4], refs[4:-1], refs[-1]
    core = scalars[0]
    for source in range(2):
        half = core if source == 0 else 1 - core
        for side in range(2):
            for i in range(4):
                off = scalars[2 + side] ^ i
                at = off ^ (off >> 1)
                rows = slice(side * 256 + i * 64, side * 256 + i * 64 + 64)
                for h in range(2):
                    block_ref[half, rows, h * 128:(h + 1) * 128] = pieces[2 * source + side][at, 0, h * 64:(h + 1) * 64]
    gots = refs[:3 - panel]
    got = sum(g[...] for g in gots)
    state = state_ref[...] - dot(block_ref[0], got[:256]) - dot(block_ref[1], got[256:])
    next_ref, new_ref = refs[3 - panel:]
    next_ref[...] = state
    new_ref[...] = solve(high_ref, low_ref, state)


def step(scalars, state, inverse, factor=None, panel=None, more=()):
    full = lambda shape: pl.BlockSpec(shape, lambda i, s: (0, 0))
    part = pl.BlockSpec((4, 1, 128, 128), lambda i, s: (0, panel, 0, 0))
    tall, square = full((512, 128)), full((512, 512))
    shapes = [jax.ShapeDtypeStruct((512, 128), BF)]
    scratch = []
    if panel is None:
        kernel, ins, factor = first_kernel, [], ()
    else:
        kernel, ins = lambda *refs: step_kernel(panel, *refs), [part] * 4 + [tall] * len(more)
        scratch = [pltpu.VMEM((2, 512, 256), BF)]
        shapes = [jax.ShapeDtypeStruct((512, 128), F32)] + shapes
    return pl.pallas_call(
        kernel,
        grid_spec=pltpu.PrefetchScalarGridSpec(
            num_scalar_prefetch=1,
            grid=(1,),
            in_specs=[tall, square, square] + ins,
            out_specs=[full(v.shape) for v in shapes],
            scratch_shapes=scratch,
        ),
        out_shape=shapes,
        compiler_params=pltpu.CompilerParams(vmem_limit_bytes=32 << 20),
    )(scalars, state, *inverse, *factor, *more)


def update_kernel(scalars, mine_ref, other_ref, rhs_ref, early_ref, *rest):
    near, far, out_ref, sent_ref = rest[:8], rest[8:16], rest[16], rest[17]
    j = pl.program_id(0)
    place, core = scalars[64], scalars[65]

    def rows(panel, half, size=256):
        return pl.ds(pl.multiple_of((core ^ (half // 256)) * 1024 + panel * 256 + half % 256, 128), size)

    def put(part_ref, p, lanes):
        for u in range(3):
            row = 512 + p * 384 + u * 128
            sent_ref[rows(row // 512, row % 512, 128), lanes] = part_ref[0, u * 128:(u + 1) * 128]

    for h in range(2):
        lanes = slice(h * 128, (h + 1) * 128)
        for half in (0, 256):
            sent_ref[rows(0, half), lanes] = early_ref[h, half:half + 256]
        for p in range(4):
            low = scalars[p * 16 + 2 * j + h] < 8

            @pl.when(low)
            def _():
                put(near[p * 2 + h], p, lanes)

            @pl.when(jnp.logical_not(low))
            def _():
                put(far[p * 2 + h], p, lanes)
    dot = lambda a, b: jnp.dot(a, b, preferred_element_type=F32)
    for c in range(2):
        out_ref[c] = rhs_ref[c] - (dot(mine_ref[c], sent_ref[:1024]) + dot(other_ref[c], sent_ref[1024:]))

    @pl.when(place < 4)
    def _():
        for half in (0, 256):
            out_ref[0, half:half + 256] = sent_ref[rows(place, half), :].astype(F32)


def update(scalars, mine, other, rhs, early, near, far):
    cycles, tile, depth = mine.shape
    pairs = [(p, h) for p in range(4) for h in range(2)]
    near_specs = [
        pl.BlockSpec((1, 384, 128), lambda j, s, p=p, h=h: (jnp.minimum(s[p * 16 + 2 * j + h], 7), 0, 0))
        for p, h in pairs
    ]
    far_specs = [
        pl.BlockSpec((1, 384, 128), lambda j, s, p=p, h=h: (jnp.maximum(s[p * 16 + 2 * j + h] - 8, 0), 0, 0))
        for p, h in pairs
    ]
    return pl.pallas_call(
        update_kernel,
        grid_spec=pltpu.PrefetchScalarGridSpec(
            num_scalar_prefetch=1,
            grid=(rhs.shape[2] // 256,),
            in_specs=[
                pl.BlockSpec((cycles, tile, depth), lambda j, s: (0, 0, 0)),
                pl.BlockSpec((cycles, tile, depth), lambda j, s: (0, 0, 0)),
                pl.BlockSpec((cycles, tile, 256), lambda j, s: (0, 0, j)),
                pl.BlockSpec((2, 512, 128), lambda j, s: (j, 0, 0)),
            ] + near_specs + far_specs,
            out_specs=pl.BlockSpec((cycles, tile, 256), lambda j, s: (0, 0, j)),
            scratch_shapes=[pltpu.VMEM((2048, 256), BF)],
        ),
        out_shape=jax.ShapeDtypeStruct(rhs.shape, F32),
        compiler_params=pltpu.CompilerParams(vmem_limit_bytes=48 << 20),
    )(scalars, mine, other, rhs, early, *[near[p] for p, _ in pairs], *[far[p] for p, _ in pairs])


def local(rhs, factor, inverses):
    x, y, z = (lax.axis_index(a) for a in ("x", "y", "z"))
    core = lax.axis_index("rhs")
    place = (y * 4 + z) * 4 + x
    owner = place < 4
    zero = jnp.zeros((), BF)

    slabs = loads(rhs, factor[0].reshape(1, 512, 1024))
    outward = {
        (p, d): permute(slabs[4 * p + d], [((i, 0, 0), (i, 0, d) if p else (i, d, 0)) for i in range(4)])
        for p, d in ((0, 3), (0, 1), (1, 1), (0, 2), (1, 2), (1, 3))
    }
    hold_a = jnp.where(owner, slabs[0], zero) + outward[0, 1] + outward[0, 2] + outward[0, 3]
    own_b, hold_a = lax.optimization_barrier((slabs[4], hold_a))
    hold_b = jnp.where(owner, own_b, zero) + outward[1, 1] + outward[1, 2] + outward[1, 3]

    def finish(hold, axis):
        tail = [hold[512:, k * 128:(k + 1) * 128] for k in range(4)]
        message = lambda d: jnp.concatenate([hold[:512, d * 128:(d + 1) * 128]] + tail, axis=0)
        mine = jnp.where((z if axis == "y" else y) == 0, message(0), zero)
        for d in (1, 3, 2):
            if axis == "y":
                moves = [((i, j, 0), (i, j, d)) for i in range(4) for j in range(4)]
            else:
                moves = [((i, 0, j), (i, d, j)) for i in range(4) for j in range(4)]
            mine = mine + permute(message(d), moves)
        return mine

    mine_a = finish(hold_a, "y")
    mine_b = finish(hold_b, "z")

    inverse = lax.dynamic_index_in_dim(inverses, x, 0, keepdims=False)
    rounded = lax.reduce_precision(inverse, 8, 7)
    inverse = (rounded.astype(BF), (inverse - rounded).astype(BF))
    where = jnp.stack([core, x, y, z]).astype(jnp.int32)
    state = mine_a[:512].astype(F32) + mine_b[:512].astype(F32)
    state, *inverse = lax.optimization_barrier((state, *inverse))
    sent_0, = step(where, state, inverse)
    gots = [hop(sent_0, (0, 1)), hop(sent_0, (0, 3)), hop(sent_0, (0, 2))]

    piece_a, piece_b, _ = lax.optimization_barrier((mine_a[512:], mine_b[512:], sent_0))
    near_a, near_b = swap(piece_a, "y", 1), swap(piece_b, "z", 1)
    near_a, near_b, *gots = lax.optimization_barrier((near_a, near_b, *gots))

    def complete(piece, near, axis):
        two = jnp.stack([piece, near])
        return jnp.concatenate([two, swap(two, axis, 3)], axis=0).reshape(4, 3, 128, 128)

    top, bottom = complete(piece_a, near_a, "y"), complete(piece_b, near_b, "z")
    block = (top, bottom, lax.ppermute(top, "rhs", [(0, 1), (1, 0)]), lax.ppermute(bottom, "rhs", [(0, 1), (1, 0)]))

    panel_0 = jnp.where(x == 0, sent_0, gots[0] + gots[1] + gots[2])
    early_0 = lax.all_gather(panel_0, ("y", "z"), axis=0)
    state, sent_1 = step(where, state, inverse, block, 0, gots)
    gots_1 = [hop(sent_1, (1, 2)), hop(sent_1, (1, 3))]
    state, sent_2 = step(where, state, inverse, block, 1, gots_1)
    got = hop(sent_2, (2, 3))
    state, sent = step(where, state, inverse, block, 2, (got,))
    sent_2 = jnp.where(x == 2, sent_2, sent_1)
    sent = jnp.where(x == 3, sent, sent_2)
    back = hop(sent, (1, 0), (2, 1), (3, 2))
    far = hop(sent, (2, 0), (3, 1))
    wrap = hop(sent, (3, 0))
    panel_1 = jnp.where(x == 1, sent, jnp.where(x == 0, back, gots_1[0] + gots_1[1]))
    panel_2 = jnp.where(x == 2, sent, jnp.where(x == 3, got, jnp.where(x == 1, back, far)))
    panel_3 = jnp.where(x == 3, sent, jnp.where(x == 2, back, jnp.where(x == 1, far, wrap)))
    cat = lambda *v: jnp.concatenate(v, axis=0)
    parts = [panel_1[:384], cat(panel_1[384:], panel_2[:256]), cat(panel_2[256:], panel_3[:128]), panel_3[128:]]
    flat_factor = factor.reshape(2, 512, 1024)
    other_factor = lax.ppermute(flat_factor, "rhs", [(0, 1), (1, 0)])
    near, early_0, other_factor, far_late = spread(parts, early_0, other_factor)
    scalars = jnp.concatenate([places(y, z), jnp.stack([place, core])]).astype(jnp.int32)
    return update(scalars, flat_factor, other_factor, rhs, early_0, near, far_late)


def solution(mesh):
    grid = Mesh(mesh.devices.reshape(4, 4, 4, 2), ("y", "z", "x", "rhs"))
    return jax.shard_map(
        local,
        mesh=grid,
        in_specs=(P(None, ROWS, "rhs"), P(None, ROWS, None, "rhs"), P()),
        out_specs=P(None, ROWS, "rhs"),
        check_vma=False,
    )
```

```python
import jax
import jax.numpy as jnp
from jax import lax
from jax.experimental import pallas as pl
from jax.experimental.pallas import tpu as pltpu
from jax.sharding import Mesh, PartitionSpec as P

ROWS = ("y", "z", "x")
BF = jnp.bfloat16
F32 = jnp.float32
ALL = [(j, k) for j in range(4) for k in range(4)]
ORDERS = (
    (("y", 1), ("y", 3), ("z", 1), ("z", 3)),
    (("y", 3), ("y", 1), ("z", 3), ("z", 1)),
    (("z", 1), ("z", 3), ("y", 1), ("y", 3)),
    (("z", 3), ("z", 1), ("y", 3), ("y", 1)),
)


def flat(x, y, z):
    return ((y % 4) * 4 + (z % 4)) * 4 + (x % 4)


def permute(value, moves):
    return lax.ppermute(value, ROWS, [(flat(*a), flat(*b)) for a, b in moves])


def hop(value, *planes):
    return permute(value, [((a, j, k), (b, j, k)) for a, b in planes for j, k in ALL])


def swap(value, axis, flip):
    return lax.ppermute(value, axis, [(i, i ^ flip) for i in range(4)])


def spread(parts, early, other):
    parts = [p[None] for p in parts]
    for step in range(3):
        got = [swap(p, *order[step]) for p, order in zip(parts, ORDERS)]
        if step == 0:
            early, got[3] = lax.optimization_barrier((early, got[3]))
        parts = [jnp.concatenate([p, g], axis=0) for p, g in zip(parts, got)]
    got = [swap(p, *order[3]) for p, order in zip(parts, ORDERS)]
    other, *got = lax.optimization_barrier((other, *got))
    return parts, early, other, got


def places(y, z):
    sites = jnp.arange(16, dtype=jnp.int32)
    tables = []
    for order in ORDERS:
        off = {"y": (sites // 4) ^ y, "z": (sites % 4) ^ z}
        total = jnp.zeros_like(sites)
        for step, (axis, flip) in enumerate(order):
            o = off[axis]
            upper = o >> 1
            bit = upper if flip == 3 else (o & 1) ^ upper
            total = total + (bit << step)
        tables.append(total)
    return jnp.stack(tables).reshape(-1)


def split(value):
    high = value.astype(BF)
    return high, (value - high.astype(F32)).astype(BF)


def put_piece(factor_ref, base, out_ref):
    for u in range(12):
        rows = slice(base + u % 2 * 32, base + u % 2 * 32 + 32)
        at = 512 + u % 3 * 32
        out_ref[at:at + 32, u // 3 * 128:(u // 3 + 1) * 128] = factor_ref[0, rows, u // 2 * 128:(u // 2 + 1) * 128]


def load_kernel(rhs_ref, factor_ref, *outs):
    for d in range(4):
        for j in range(4):
            lanes = slice(j * 128, (j + 1) * 128)
            at = d * 512 + j * 128
            outs[d][:512, lanes] = rhs_ref[0, :, at:at + 128].astype(BF)
            at = j * 512 + d * 128
            outs[4 + d][:512, lanes] = split(rhs_ref[0, :, at:at + 128])[1]
        put_piece(factor_ref, d * 64, outs[d])
        put_piece(factor_ref, 256 + d * 64, outs[4 + d])


def loads(rhs, factor):
    return pl.pallas_call(
        load_kernel,
        grid=(1,),
        in_specs=[pl.BlockSpec((1, 512, 2048), lambda i: (0, 0, 0)), pl.BlockSpec((1, 512, 1024), lambda i: (0, 0, 0))],
        out_specs=[pl.BlockSpec((608, 512), lambda i: (0, 0))] * 8,
        out_shape=[jax.ShapeDtypeStruct((608, 512), BF)] * 8,
        compiler_params=pltpu.CompilerParams(vmem_limit_bytes=48 << 20),
    )(rhs, factor)


def solve(high_ref, low_ref, state):
    high, low = split(state)
    dot = lambda a, b: jnp.dot(a, b, preferred_element_type=F32)
    return (dot(high_ref[...], high) + dot(high_ref[...], low) + dot(low_ref[...], high)).astype(BF)


def first_kernel(scalars, state_ref, high_ref, low_ref, sent_ref):
    sent_ref[...] = solve(high_ref, low_ref, state_ref[...])


def step_kernel(panel, scalars, state_ref, high_ref, low_ref, *refs):
    dot = lambda a, b: jnp.dot(a, b, preferred_element_type=F32)
    pieces, refs, block_ref = refs[:4], refs[4:-1], refs[-1]
    core = scalars[0]
    for source in range(2):
        half = core if source == 0 else 1 - core
        for side in range(2):
            for i in range(4):
                off = scalars[2 + side] ^ i
                at = off ^ (off >> 1)
                rows = slice(side * 256 + i * 64, side * 256 + i * 64 + 64)
                for h in range(2):
                    block_ref[half, rows, h * 128:(h + 1) * 128] = pieces[2 * source + side][at, 0, h * 64:(h + 1) * 64]
    gots = refs[:3 - panel]
    got = sum(g[...] for g in gots)
    state = state_ref[...] - dot(block_ref[0], got[:256]) - dot(block_ref[1], got[256:])
    next_ref, new_ref = refs[3 - panel:]
    next_ref[...] = state
    new_ref[...] = solve(high_ref, low_ref, state)


def step(scalars, state, inverse, factor=None, panel=None, more=()):
    full = lambda shape: pl.BlockSpec(shape, lambda i, s: (0, 0))
    part = pl.BlockSpec((4, 1, 128, 128), lambda i, s: (0, panel, 0, 0))
    tall, square = full((512, 128)), full((512, 512))
    shapes = [jax.ShapeDtypeStruct((512, 128), BF)]
    scratch = []
    if panel is None:
        kernel, ins, factor = first_kernel, [], ()
    else:
        kernel, ins = lambda *refs: step_kernel(panel, *refs), [part] * 4 + [tall] * len(more)
        scratch = [pltpu.VMEM((2, 512, 256), BF)]
        shapes = [jax.ShapeDtypeStruct((512, 128), F32)] + shapes
    return pl.pallas_call(
        kernel,
        grid_spec=pltpu.PrefetchScalarGridSpec(
            num_scalar_prefetch=1,
            grid=(1,),
            in_specs=[tall, square, square] + ins,
            out_specs=[full(v.shape) for v in shapes],
            scratch_shapes=scratch,
        ),
        out_shape=shapes,
        compiler_params=pltpu.CompilerParams(vmem_limit_bytes=32 << 20),
    )(scalars, state, *inverse, *factor, *more)


def update_kernel(scalars, mine_ref, other_ref, rhs_ref, early_ref, *rest):
    near, far, out_ref, sent_ref = rest[:8], rest[8:16], rest[16], rest[17]
    j = pl.program_id(0)
    place, core = scalars[64], scalars[65]

    def rows(panel, half, size=256):
        return pl.ds(pl.multiple_of((core ^ (half // 256)) * 1024 + panel * 256 + half % 256, 128), size)

    def put(part_ref, p, lanes):
        for u in range(3):
            row = 512 + p * 384 + u * 128
            sent_ref[rows(row // 512, row % 512, 128), lanes] = part_ref[0, u * 128:(u + 1) * 128]

    for h in range(2):
        lanes = slice(h * 128, (h + 1) * 128)
        for half in (0, 256):
            sent_ref[rows(0, half), lanes] = early_ref[h, half:half + 256]
        for p in range(4):
            low = scalars[p * 16 + 2 * j + h] < 8

            @pl.when(low)
            def _():
                put(near[p * 2 + h], p, lanes)

            @pl.when(jnp.logical_not(low))
            def _():
                put(far[p * 2 + h], p, lanes)
    dot = lambda a, b: jnp.dot(a, b, preferred_element_type=F32)
    for c in range(2):
        out_ref[c] = rhs_ref[c] - (dot(mine_ref[c], sent_ref[:1024]) + dot(other_ref[c], sent_ref[1024:]))

    @pl.when(place < 4)
    def _():
        for half in (0, 256):
            out_ref[0, half:half + 256] = sent_ref[rows(place, half), :].astype(F32)


def update(scalars, mine, other, rhs, early, near, far):
    cycles, tile, depth = mine.shape
    pairs = [(p, h) for p in range(4) for h in range(2)]
    near_specs = [
        pl.BlockSpec((1, 384, 128), lambda j, s, p=p, h=h: (jnp.minimum(s[p * 16 + 2 * j + h], 7), 0, 0))
        for p, h in pairs
    ]
    far_specs = [
        pl.BlockSpec((1, 384, 128), lambda j, s, p=p, h=h: (jnp.maximum(s[p * 16 + 2 * j + h] - 8, 0), 0, 0))
        for p, h in pairs
    ]
    return pl.pallas_call(
        update_kernel,
        grid_spec=pltpu.PrefetchScalarGridSpec(
            num_scalar_prefetch=1,
            grid=(rhs.shape[2] // 256,),
            in_specs=[
                pl.BlockSpec((cycles, tile, depth), lambda j, s: (0, 0, 0)),
                pl.BlockSpec((cycles, tile, depth), lambda j, s: (0, 0, 0)),
                pl.BlockSpec((cycles, tile, 256), lambda j, s: (0, 0, j)),
                pl.BlockSpec((2, 512, 128), lambda j, s: (j, 0, 0)),
            ] + near_specs + far_specs,
            out_specs=pl.BlockSpec((cycles, tile, 256), lambda j, s: (0, 0, j)),
            scratch_shapes=[pltpu.VMEM((2048, 256), BF)],
        ),
        out_shape=jax.ShapeDtypeStruct(rhs.shape, F32),
        compiler_params=pltpu.CompilerParams(vmem_limit_bytes=48 << 20),
    )(scalars, mine, other, rhs, early, *[near[p] for p, _ in pairs], *[far[p] for p, _ in pairs])


def local(rhs, factor, inverses):
    x, y, z = (lax.axis_index(a) for a in ("x", "y", "z"))
    core = lax.axis_index("rhs")
    place = (y * 4 + z) * 4 + x
    owner = place < 4
    zero = jnp.zeros((), BF)

    slabs = loads(rhs, factor[0].reshape(1, 512, 1024))
    outward = {
        (p, d): permute(slabs[4 * p + d], [((i, 0, 0), (i, 0, d) if p else (i, d, 0)) for i in range(4)])
        for p, d in ((0, 3), (0, 1), (1, 1), (0, 2), (1, 2), (1, 3))
    }
    hold_a = jnp.where(owner, slabs[0], zero) + outward[0, 1] + outward[0, 2] + outward[0, 3]
    own_b, hold_a = lax.optimization_barrier((slabs[4], hold_a))
    hold_b = jnp.where(owner, own_b, zero) + outward[1, 1] + outward[1, 2] + outward[1, 3]

    def finish(hold, axis):
        tail = [hold[512:, k * 128:(k + 1) * 128] for k in range(4)]
        message = lambda d: jnp.concatenate([hold[:512, d * 128:(d + 1) * 128]] + tail, axis=0)
        mine = jnp.where((z if axis == "y" else y) == 0, message(0), zero)
        for d in (2, 1, 3):
            if axis == "y":
                moves = [((i, j, 0), (i, j, d)) for i in range(4) for j in range(4)]
            else:
                moves = [((i, 0, j), (i, d, j)) for i in range(4) for j in range(4)]
            mine = mine + permute(message(d), moves)
        return mine

    mine_a = finish(hold_a, "y")
    mine_b = finish(hold_b, "z")

    inverse = lax.dynamic_index_in_dim(inverses, x, 0, keepdims=False)
    rounded = lax.reduce_precision(inverse, 8, 7)
    inverse = (rounded.astype(BF), (inverse - rounded).astype(BF))
    where = jnp.stack([core, x, y, z]).astype(jnp.int32)
    state = mine_a[:512].astype(F32) + mine_b[:512].astype(F32)
    state, *inverse = lax.optimization_barrier((state, *inverse))
    sent_0, = step(where, state, inverse)
    gots = [hop(sent_0, (0, 1)), hop(sent_0, (0, 3)), hop(sent_0, (0, 2))]

    piece_a, piece_b, _ = lax.optimization_barrier((mine_a[512:], mine_b[512:], sent_0))
    near_a, near_b = swap(piece_a, "y", 1), swap(piece_b, "z", 1)
    near_a, near_b, *gots = lax.optimization_barrier((near_a, near_b, *gots))

    def complete(piece, near, axis):
        two = jnp.stack([piece, near])
        return jnp.concatenate([two, swap(two, axis, 3)], axis=0).reshape(4, 3, 128, 128)

    top, bottom = complete(piece_a, near_a, "y"), complete(piece_b, near_b, "z")
    block = (top, bottom, lax.ppermute(top, "rhs", [(0, 1), (1, 0)]), lax.ppermute(bottom, "rhs", [(0, 1), (1, 0)]))

    panel_0 = jnp.where(x == 0, sent_0, gots[0] + gots[1] + gots[2])
    early_0 = lax.all_gather(panel_0, ("y", "z"), axis=0)
    state, sent_1 = step(where, state, inverse, block, 0, gots)
    gots_1 = [hop(sent_1, (1, 2)), hop(sent_1, (1, 3))]
    state, sent_2 = step(where, state, inverse, block, 1, gots_1)
    got = hop(sent_2, (2, 3))
    state, sent = step(where, state, inverse, block, 2, (got,))
    sent_2 = jnp.where(x == 2, sent_2, sent_1)
    sent = jnp.where(x == 3, sent, sent_2)
    back = hop(sent, (1, 0), (2, 1), (3, 2))
    far = hop(sent, (2, 0), (3, 1))
    wrap = hop(sent, (3, 0))
    panel_1 = jnp.where(x == 1, sent, jnp.where(x == 0, back, gots_1[0] + gots_1[1]))
    panel_2 = jnp.where(x == 2, sent, jnp.where(x == 3, got, jnp.where(x == 1, back, far)))
    panel_3 = jnp.where(x == 3, sent, jnp.where(x == 2, back, jnp.where(x == 1, far, wrap)))
    cat = lambda *v: jnp.concatenate(v, axis=0)
    parts = [panel_1[:384], cat(panel_1[384:], panel_2[:256]), cat(panel_2[256:], panel_3[:128]), panel_3[128:]]
    flat_factor = factor.reshape(2, 512, 1024)
    other_factor = lax.ppermute(flat_factor, "rhs", [(0, 1), (1, 0)])
    near, early_0, other_factor, far_late = spread(parts, early_0, other_factor)
    scalars = jnp.concatenate([places(y, z), jnp.stack([place, core])]).astype(jnp.int32)
    return update(scalars, flat_factor, other_factor, rhs, early_0, near, far_late)


def solution(mesh):
    grid = Mesh(mesh.devices.reshape(4, 4, 4, 2), ("y", "z", "x", "rhs"))
    return jax.shard_map(
        local,
        mesh=grid,
        in_specs=(P(None, ROWS, "rhs"), P(None, ROWS, None, "rhs"), P()),
        out_specs=P(None, ROWS, "rhs"),
        check_vma=False,
    )
```

```python
import jax
import jax.numpy as jnp
from jax import lax
from jax.experimental import pallas as pl
from jax.experimental.pallas import tpu as pltpu
from jax.sharding import Mesh, PartitionSpec as P

ROWS = ("y", "z", "x")
BF = jnp.bfloat16
F32 = jnp.float32
ALL = [(j, k) for j in range(4) for k in range(4)]
ORDERS = (
    (("y", 1), ("y", 3), ("z", 1), ("z", 3)),
    (("y", 3), ("y", 1), ("z", 3), ("z", 1)),
    (("z", 1), ("z", 3), ("y", 1), ("y", 3)),
    (("z", 3), ("z", 1), ("y", 3), ("y", 1)),
)


def flat(x, y, z):
    return ((y % 4) * 4 + (z % 4)) * 4 + (x % 4)


def permute(value, moves):
    return lax.ppermute(value, ROWS, [(flat(*a), flat(*b)) for a, b in moves])


def hop(value, *planes):
    return permute(value, [((a, j, k), (b, j, k)) for a, b in planes for j, k in ALL])


def swap(value, axis, flip):
    return lax.ppermute(value, axis, [(i, i ^ flip) for i in range(4)])


def spread(parts, early, other):
    parts = [p[None] for p in parts]
    for step in range(3):
        got = [swap(p, *order[step]) for p, order in zip(parts, ORDERS)]
        if step == 0:
            early, got[3] = lax.optimization_barrier((early, got[3]))
        parts = [jnp.concatenate([p, g], axis=0) for p, g in zip(parts, got)]
    got = [swap(p, *order[3]) for p, order in zip(parts, ORDERS)]
    other, *got = lax.optimization_barrier((other, *got))
    return parts, early, other, got


def places(y, z):
    sites = jnp.arange(16, dtype=jnp.int32)
    tables = []
    for order in ORDERS:
        off = {"y": (sites // 4) ^ y, "z": (sites % 4) ^ z}
        total = jnp.zeros_like(sites)
        for step, (axis, flip) in enumerate(order):
            o = off[axis]
            upper = o >> 1
            bit = upper if flip == 3 else (o & 1) ^ upper
            total = total + (bit << step)
        tables.append(total)
    return jnp.stack(tables).reshape(-1)


def split(value):
    high = value.astype(BF)
    return high, (value - high.astype(F32)).astype(BF)


def put_piece(factor_ref, base, out_ref):
    for u in range(12):
        rows = slice(base + u % 2 * 32, base + u % 2 * 32 + 32)
        at = 512 + u % 3 * 32
        out_ref[at:at + 32, u // 3 * 128:(u // 3 + 1) * 128] = factor_ref[0, rows, u // 2 * 128:(u // 2 + 1) * 128]


def load_kernel(rhs_ref, factor_ref, *outs):
    for d in range(4):
        for j in range(4):
            lanes = slice(j * 128, (j + 1) * 128)
            at = d * 512 + j * 128
            outs[d][:512, lanes] = rhs_ref[0, :, at:at + 128].astype(BF)
            at = j * 512 + d * 128
            outs[4 + d][:512, lanes] = split(rhs_ref[0, :, at:at + 128])[1]
        put_piece(factor_ref, d * 64, outs[d])
        put_piece(factor_ref, 256 + d * 64, outs[4 + d])


def loads(rhs, factor):
    return pl.pallas_call(
        load_kernel,
        grid=(1,),
        in_specs=[pl.BlockSpec((1, 512, 2048), lambda i: (0, 0, 0)), pl.BlockSpec((1, 512, 1024), lambda i: (0, 0, 0))],
        out_specs=[pl.BlockSpec((608, 512), lambda i: (0, 0))] * 8,
        out_shape=[jax.ShapeDtypeStruct((608, 512), BF)] * 8,
        compiler_params=pltpu.CompilerParams(vmem_limit_bytes=48 << 20),
    )(rhs, factor)


def solve(high_ref, low_ref, state):
    high, low = split(state)
    dot = lambda a, b: jnp.dot(a, b, preferred_element_type=F32)
    return (dot(high_ref[...], high) + dot(high_ref[...], low) + dot(low_ref[...], high)).astype(BF)


def first_kernel(scalars, state_ref, high_ref, low_ref, sent_ref):
    sent_ref[...] = solve(high_ref, low_ref, state_ref[...])


def step_kernel(panel, scalars, state_ref, high_ref, low_ref, *refs):
    dot = lambda a, b: jnp.dot(a, b, preferred_element_type=F32)
    pieces, refs, block_ref = refs[:4], refs[4:-1], refs[-1]
    core = scalars[0]
    for source in range(2):
        half = core if source == 0 else 1 - core
        for side in range(2):
            for i in range(4):
                off = scalars[2 + side] ^ i
                at = off ^ (off >> 1)
                rows = slice(side * 256 + i * 64, side * 256 + i * 64 + 64)
                for h in range(2):
                    block_ref[half, rows, h * 128:(h + 1) * 128] = pieces[2 * source + side][at, 0, h * 64:(h + 1) * 64]
    gots = refs[:3 - panel]
    got = sum(g[...] for g in gots)
    state = state_ref[...] - dot(block_ref[0], got[:256]) - dot(block_ref[1], got[256:])
    next_ref, new_ref = refs[3 - panel:]
    next_ref[...] = state
    new_ref[...] = solve(high_ref, low_ref, state)


def step(scalars, state, inverse, factor=None, panel=None, more=()):
    full = lambda shape: pl.BlockSpec(shape, lambda i, s: (0, 0))
    part = pl.BlockSpec((4, 1, 128, 128), lambda i, s: (0, panel, 0, 0))
    tall, square = full((512, 128)), full((512, 512))
    shapes = [jax.ShapeDtypeStruct((512, 128), BF)]
    scratch = []
    if panel is None:
        kernel, ins, factor = first_kernel, [], ()
    else:
        kernel, ins = lambda *refs: step_kernel(panel, *refs), [part] * 4 + [tall] * len(more)
        scratch = [pltpu.VMEM((2, 512, 256), BF)]
        shapes = [jax.ShapeDtypeStruct((512, 128), F32)] + shapes
    return pl.pallas_call(
        kernel,
        grid_spec=pltpu.PrefetchScalarGridSpec(
            num_scalar_prefetch=1,
            grid=(1,),
            in_specs=[tall, square, square] + ins,
            out_specs=[full(v.shape) for v in shapes],
            scratch_shapes=scratch,
        ),
        out_shape=shapes,
        compiler_params=pltpu.CompilerParams(vmem_limit_bytes=32 << 20),
    )(scalars, state, *inverse, *factor, *more)


def update_kernel(scalars, mine_ref, other_ref, rhs_ref, early_ref, *rest):
    near, far, out_ref, sent_ref = rest[:8], rest[8:16], rest[16], rest[17]
    j = pl.program_id(0)
    place, core = scalars[64], scalars[65]

    def rows(panel, half, size=256):
        return pl.ds(pl.multiple_of((core ^ (half // 256)) * 1024 + panel * 256 + half % 256, 128), size)

    def put(part_ref, p, lanes):
        for u in range(3):
            row = 512 + p * 384 + u * 128
            sent_ref[rows(row // 512, row % 512, 128), lanes] = part_ref[0, u * 128:(u + 1) * 128]

    for h in range(2):
        lanes = slice(h * 128, (h + 1) * 128)
        for half in (0, 256):
            sent_ref[rows(0, half), lanes] = early_ref[h, half:half + 256]
        for p in range(4):
            low = scalars[p * 16 + 2 * j + h] < 8

            @pl.when(low)
            def _():
                put(near[p * 2 + h], p, lanes)

            @pl.when(jnp.logical_not(low))
            def _():
                put(far[p * 2 + h], p, lanes)
    dot = lambda a, b: jnp.dot(a, b, preferred_element_type=F32)
    for c in range(2):
        out_ref[c] = rhs_ref[c] - (dot(mine_ref[c], sent_ref[:1024]) + dot(other_ref[c], sent_ref[1024:]))

    @pl.when(place < 4)
    def _():
        for half in (0, 256):
            out_ref[0, half:half + 256] = sent_ref[rows(place, half), :].astype(F32)


def update(scalars, mine, other, rhs, early, near, far):
    cycles, tile, depth = mine.shape
    pairs = [(p, h) for p in range(4) for h in range(2)]
    near_specs = [
        pl.BlockSpec((1, 384, 128), lambda j, s, p=p, h=h: (jnp.minimum(s[p * 16 + 2 * j + h], 7), 0, 0))
        for p, h in pairs
    ]
    far_specs = [
        pl.BlockSpec((1, 384, 128), lambda j, s, p=p, h=h: (jnp.maximum(s[p * 16 + 2 * j + h] - 8, 0), 0, 0))
        for p, h in pairs
    ]
    return pl.pallas_call(
        update_kernel,
        grid_spec=pltpu.PrefetchScalarGridSpec(
            num_scalar_prefetch=1,
            grid=(rhs.shape[2] // 256,),
            in_specs=[
                pl.BlockSpec((cycles, tile, depth), lambda j, s: (0, 0, 0)),
                pl.BlockSpec((cycles, tile, depth), lambda j, s: (0, 0, 0)),
                pl.BlockSpec((cycles, tile, 256), lambda j, s: (0, 0, j)),
                pl.BlockSpec((2, 512, 128), lambda j, s: (j, 0, 0)),
            ] + near_specs + far_specs,
            out_specs=pl.BlockSpec((cycles, tile, 256), lambda j, s: (0, 0, j)),
            scratch_shapes=[pltpu.VMEM((2048, 256), BF)],
        ),
        out_shape=jax.ShapeDtypeStruct(rhs.shape, F32),
        compiler_params=pltpu.CompilerParams(vmem_limit_bytes=48 << 20),
    )(scalars, mine, other, rhs, early, *[near[p] for p, _ in pairs], *[far[p] for p, _ in pairs])


def local(rhs, factor, inverses):
    x, y, z = (lax.axis_index(a) for a in ("x", "y", "z"))
    core = lax.axis_index("rhs")
    place = (y * 4 + z) * 4 + x
    owner = place < 4
    zero = jnp.zeros((), BF)

    slabs = loads(rhs, factor[0].reshape(1, 512, 1024))
    outward = {
        (p, d): permute(slabs[4 * p + d], [((i, 0, 0), (i, 0, d) if p else (i, d, 0)) for i in range(4)])
        for p, d in ((0, 3), (0, 2), (1, 2), (0, 1), (1, 1), (1, 3))
    }
    hold_a = jnp.where(owner, slabs[0], zero) + outward[0, 1] + outward[0, 2] + outward[0, 3]
    own_b, hold_a = lax.optimization_barrier((slabs[4], hold_a))
    hold_b = jnp.where(owner, own_b, zero) + outward[1, 1] + outward[1, 2] + outward[1, 3]

    def finish(hold, axis):
        tail = [hold[512:, k * 128:(k + 1) * 128] for k in range(4)]
        message = lambda d: jnp.concatenate([hold[:512, d * 128:(d + 1) * 128]] + tail, axis=0)
        mine = jnp.where((z if axis == "y" else y) == 0, message(0), zero)
        for d in (2, 1, 3):
            if axis == "y":
                moves = [((i, j, 0), (i, j, d)) for i in range(4) for j in range(4)]
            else:
                moves = [((i, 0, j), (i, d, j)) for i in range(4) for j in range(4)]
            mine = mine + permute(message(d), moves)
        return mine

    mine_a = finish(hold_a, "y")
    mine_b = finish(hold_b, "z")

    inverse = lax.dynamic_index_in_dim(inverses, x, 0, keepdims=False)
    rounded = lax.reduce_precision(inverse, 8, 7)
    inverse = (rounded.astype(BF), (inverse - rounded).astype(BF))
    where = jnp.stack([core, x, y, z]).astype(jnp.int32)
    state = mine_a[:512].astype(F32) + mine_b[:512].astype(F32)
    state, *inverse = lax.optimization_barrier((state, *inverse))
    sent_0, = step(where, state, inverse)
    gots = [hop(sent_0, (0, 1)), hop(sent_0, (0, 3)), hop(sent_0, (0, 2))]

    piece_a, piece_b, _ = lax.optimization_barrier((mine_a[512:], mine_b[512:], sent_0))
    near_a, near_b = swap(piece_a, "y", 1), swap(piece_b, "z", 1)
    near_a, near_b, *gots = lax.optimization_barrier((near_a, near_b, *gots))

    def complete(piece, near, axis):
        two = jnp.stack([piece, near])
        return jnp.concatenate([two, swap(two, axis, 3)], axis=0).reshape(4, 3, 128, 128)

    top, bottom = complete(piece_a, near_a, "y"), complete(piece_b, near_b, "z")
    block = (top, bottom, lax.ppermute(top, "rhs", [(0, 1), (1, 0)]), lax.ppermute(bottom, "rhs", [(0, 1), (1, 0)]))

    panel_0 = jnp.where(x == 0, sent_0, gots[0] + gots[1] + gots[2])
    early_0 = lax.all_gather(panel_0, ("y", "z"), axis=0)
    state, sent_1 = step(where, state, inverse, block, 0, gots)
    gots_1 = [hop(sent_1, (1, 2)), hop(sent_1, (1, 3))]
    state, sent_2 = step(where, state, inverse, block, 1, gots_1)
    got = hop(sent_2, (2, 3))
    state, sent = step(where, state, inverse, block, 2, (got,))
    sent_2 = jnp.where(x == 2, sent_2, sent_1)
    sent = jnp.where(x == 3, sent, sent_2)
    back = hop(sent, (1, 0), (2, 1), (3, 2))
    far = hop(sent, (2, 0), (3, 1))
    wrap = hop(sent, (3, 0))
    panel_1 = jnp.where(x == 1, sent, jnp.where(x == 0, back, gots_1[0] + gots_1[1]))
    panel_2 = jnp.where(x == 2, sent, jnp.where(x == 3, got, jnp.where(x == 1, back, far)))
    panel_3 = jnp.where(x == 3, sent, jnp.where(x == 2, back, jnp.where(x == 1, far, wrap)))
    cat = lambda *v: jnp.concatenate(v, axis=0)
    parts = [panel_1[:384], cat(panel_1[384:], panel_2[:256]), cat(panel_2[256:], panel_3[:128]), panel_3[128:]]
    flat_factor = factor.reshape(2, 512, 1024)
    other_factor = lax.ppermute(flat_factor, "rhs", [(0, 1), (1, 0)])
    near, early_0, other_factor, far_late = spread(parts, early_0, other_factor)
    scalars = jnp.concatenate([places(y, z), jnp.stack([place, core])]).astype(jnp.int32)
    return update(scalars, flat_factor, other_factor, rhs, early_0, near, far_late)


def solution(mesh):
    grid = Mesh(mesh.devices.reshape(4, 4, 4, 2), ("y", "z", "x", "rhs"))
    return jax.shard_map(
        local,
        mesh=grid,
        in_specs=(P(None, ROWS, "rhs"), P(None, ROWS, None, "rhs"), P()),
        out_specs=P(None, ROWS, "rhs"),
        check_vma=False,
    )
```

```python
import jax
import jax.numpy as jnp
from jax import lax
from jax.experimental import pallas as pl
from jax.experimental.pallas import tpu as pltpu
from jax.sharding import Mesh, PartitionSpec as P

ROWS = ("y", "z", "x")
BF = jnp.bfloat16
F32 = jnp.float32
ALL = [(j, k) for j in range(4) for k in range(4)]
ORDERS = (
    (("y", 1), ("y", 3), ("z", 1), ("z", 3)),
    (("y", 3), ("y", 1), ("z", 3), ("z", 1)),
    (("z", 1), ("z", 3), ("y", 1), ("y", 3)),
    (("z", 3), ("z", 1), ("y", 3), ("y", 1)),
)


def flat(x, y, z):
    return ((y % 4) * 4 + (z % 4)) * 4 + (x % 4)


def permute(value, moves):
    return lax.ppermute(value, ROWS, [(flat(*a), flat(*b)) for a, b in moves])


def hop(value, *planes):
    return permute(value, [((a, j, k), (b, j, k)) for a, b in planes for j, k in ALL])


def swap(value, axis, flip):
    return lax.ppermute(value, axis, [(i, i ^ flip) for i in range(4)])


def spread(parts, early, other):
    parts = [p[None] for p in parts]
    for step in range(3):
        got = [swap(p, *order[step]) for p, order in zip(parts, ORDERS)]
        if step == 0:
            early, got[3] = lax.optimization_barrier((early, got[3]))
        parts = [jnp.concatenate([p, g], axis=0) for p, g in zip(parts, got)]
    got = [swap(p, *order[3]) for p, order in zip(parts, ORDERS)]
    other, *got = lax.optimization_barrier((other, *got))
    return parts, early, other, got


def places(y, z):
    sites = jnp.arange(16, dtype=jnp.int32)
    tables = []
    for order in ORDERS:
        off = {"y": (sites // 4) ^ y, "z": (sites % 4) ^ z}
        total = jnp.zeros_like(sites)
        for step, (axis, flip) in enumerate(order):
            o = off[axis]
            upper = o >> 1
            bit = upper if flip == 3 else (o & 1) ^ upper
            total = total + (bit << step)
        tables.append(total)
    return jnp.stack(tables).reshape(-1)


def split(value):
    high = value.astype(BF)
    return high, (value - high.astype(F32)).astype(BF)


def put_piece(factor_ref, base, out_ref):
    for u in range(12):
        rows = slice(base + u % 2 * 32, base + u % 2 * 32 + 32)
        at = 512 + u % 3 * 32
        out_ref[at:at + 32, u // 3 * 128:(u // 3 + 1) * 128] = factor_ref[0, rows, u // 2 * 128:(u // 2 + 1) * 128]


def load_kernel(rhs_ref, factor_ref, *outs):
    for d in range(4):
        for j in range(4):
            lanes = slice(j * 128, (j + 1) * 128)
            at = d * 512 + j * 128
            outs[d][:512, lanes] = rhs_ref[0, :, at:at + 128].astype(BF)
            at = j * 512 + d * 128
            outs[4 + d][:512, lanes] = split(rhs_ref[0, :, at:at + 128])[1]
        put_piece(factor_ref, d * 64, outs[d])
        put_piece(factor_ref, 256 + d * 64, outs[4 + d])


def loads(rhs, factor):
    return pl.pallas_call(
        load_kernel,
        grid=(1,),
        in_specs=[pl.BlockSpec((1, 512, 2048), lambda i: (0, 0, 0)), pl.BlockSpec((1, 512, 1024), lambda i: (0, 0, 0))],
        out_specs=[pl.BlockSpec((608, 512), lambda i: (0, 0))] * 8,
        out_shape=[jax.ShapeDtypeStruct((608, 512), BF)] * 8,
        compiler_params=pltpu.CompilerParams(vmem_limit_bytes=48 << 20),
    )(rhs, factor)


def solve(high_ref, low_ref, state):
    high, low = split(state)
    dot = lambda a, b: jnp.dot(a, b, preferred_element_type=F32)
    return (dot(high_ref[...], high) + dot(high_ref[...], low) + dot(low_ref[...], high)).astype(BF)


def first_kernel(scalars, state_ref, high_ref, low_ref, sent_ref):
    sent_ref[...] = solve(high_ref, low_ref, state_ref[...])


def step_kernel(panel, scalars, state_ref, high_ref, low_ref, *refs):
    dot = lambda a, b: jnp.dot(a, b, preferred_element_type=F32)
    pieces, refs, block_ref = refs[:4], refs[4:-1], refs[-1]
    core = scalars[0]
    for source in range(2):
        half = core if source == 0 else 1 - core
        for side in range(2):
            for i in range(4):
                off = scalars[2 + side] ^ i
                at = off ^ (off >> 1)
                rows = slice(side * 256 + i * 64, side * 256 + i * 64 + 64)
                for h in range(2):
                    block_ref[half, rows, h * 128:(h + 1) * 128] = pieces[2 * source + side][at, 0, h * 64:(h + 1) * 64]
    gots = refs[:3 - panel]
    got = sum(g[...] for g in gots)
    state = state_ref[...] - dot(block_ref[0], got[:256]) - dot(block_ref[1], got[256:])
    next_ref, new_ref = refs[3 - panel:]
    next_ref[...] = state
    new_ref[...] = solve(high_ref, low_ref, state)


def step(scalars, state, inverse, factor=None, panel=None, more=()):
    full = lambda shape: pl.BlockSpec(shape, lambda i, s: (0, 0))
    part = pl.BlockSpec((4, 1, 128, 128), lambda i, s: (0, panel, 0, 0))
    tall, square = full((512, 128)), full((512, 512))
    shapes = [jax.ShapeDtypeStruct((512, 128), BF)]
    scratch = []
    if panel is None:
        kernel, ins, factor = first_kernel, [], ()
    else:
        kernel, ins = lambda *refs: step_kernel(panel, *refs), [part] * 4 + [tall] * len(more)
        scratch = [pltpu.VMEM((2, 512, 256), BF)]
        shapes = [jax.ShapeDtypeStruct((512, 128), F32)] + shapes
    return pl.pallas_call(
        kernel,
        grid_spec=pltpu.PrefetchScalarGridSpec(
            num_scalar_prefetch=1,
            grid=(1,),
            in_specs=[tall, square, square] + ins,
            out_specs=[full(v.shape) for v in shapes],
            scratch_shapes=scratch,
        ),
        out_shape=shapes,
        compiler_params=pltpu.CompilerParams(vmem_limit_bytes=32 << 20),
    )(scalars, state, *inverse, *factor, *more)


def update_kernel(scalars, mine_ref, other_ref, rhs_ref, early_ref, *rest):
    near, far, out_ref, sent_ref = rest[:8], rest[8:16], rest[16], rest[17]
    j = pl.program_id(0)
    place, core = scalars[64], scalars[65]

    def rows(panel, half, size=256):
        return pl.ds(pl.multiple_of((core ^ (half // 256)) * 1024 + panel * 256 + half % 256, 128), size)

    def put(part_ref, p, lanes):
        for u in range(3):
            row = 512 + p * 384 + u * 128
            sent_ref[rows(row // 512, row % 512, 128), lanes] = part_ref[0, u * 128:(u + 1) * 128]

    for h in range(2):
        lanes = slice(h * 128, (h + 1) * 128)
        for half in (0, 256):
            sent_ref[rows(0, half), lanes] = early_ref[h, half:half + 256]
        for p in range(4):
            low = scalars[p * 16 + 2 * j + h] < 8

            @pl.when(low)
            def _():
                put(near[p * 2 + h], p, lanes)

            @pl.when(jnp.logical_not(low))
            def _():
                put(far[p * 2 + h], p, lanes)
    dot = lambda a, b: jnp.dot(a, b, preferred_element_type=F32)
    for c in range(2):
        out_ref[c] = rhs_ref[c] - (dot(mine_ref[c], sent_ref[:1024]) + dot(other_ref[c], sent_ref[1024:]))

    @pl.when(place < 4)
    def _():
        for half in (0, 256):
            out_ref[0, half:half + 256] = sent_ref[rows(place, half), :].astype(F32)


def update(scalars, mine, other, rhs, early, near, far):
    cycles, tile, depth = mine.shape
    pairs = [(p, h) for p in range(4) for h in range(2)]
    near_specs = [
        pl.BlockSpec((1, 384, 128), lambda j, s, p=p, h=h: (jnp.minimum(s[p * 16 + 2 * j + h], 7), 0, 0))
        for p, h in pairs
    ]
    far_specs = [
        pl.BlockSpec((1, 384, 128), lambda j, s, p=p, h=h: (jnp.maximum(s[p * 16 + 2 * j + h] - 8, 0), 0, 0))
        for p, h in pairs
    ]
    return pl.pallas_call(
        update_kernel,
        grid_spec=pltpu.PrefetchScalarGridSpec(
            num_scalar_prefetch=1,
            grid=(rhs.shape[2] // 256,),
            in_specs=[
                pl.BlockSpec((cycles, tile, depth), lambda j, s: (0, 0, 0)),
                pl.BlockSpec((cycles, tile, depth), lambda j, s: (0, 0, 0)),
                pl.BlockSpec((cycles, tile, 256), lambda j, s: (0, 0, j)),
                pl.BlockSpec((2, 512, 128), lambda j, s: (j, 0, 0)),
            ] + near_specs + far_specs,
            out_specs=pl.BlockSpec((cycles, tile, 256), lambda j, s: (0, 0, j)),
            scratch_shapes=[pltpu.VMEM((2048, 256), BF)],
        ),
        out_shape=jax.ShapeDtypeStruct(rhs.shape, F32),
        compiler_params=pltpu.CompilerParams(vmem_limit_bytes=48 << 20),
    )(scalars, mine, other, rhs, early, *[near[p] for p, _ in pairs], *[far[p] for p, _ in pairs])


def local(rhs, factor, inverses):
    x, y, z = (lax.axis_index(a) for a in ("x", "y", "z"))
    core = lax.axis_index("rhs")
    place = (y * 4 + z) * 4 + x
    owner = place < 4
    zero = jnp.zeros((), BF)

    slabs = loads(rhs, factor[0].reshape(1, 512, 1024))
    outward = {
        (p, d): permute(slabs[4 * p + d], [((i, 0, 0), (i, 0, d) if p else (i, d, 0)) for i in range(4)])
        for p, d in ((0, 3), (0, 2), (1, 2), (0, 1), (1, 1), (1, 3))
    }
    hold_a = jnp.where(owner, slabs[0], zero) + outward[0, 1] + outward[0, 2] + outward[0, 3]
    own_b, hold_a = lax.optimization_barrier((slabs[4], hold_a))
    hold_b = jnp.where(owner, own_b, zero) + outward[1, 1] + outward[1, 2] + outward[1, 3]

    def finish(hold, axis):
        tail = [hold[512:, k * 128:(k + 1) * 128] for k in range(4)]
        message = lambda d: jnp.concatenate([hold[:512, d * 128:(d + 1) * 128]] + tail, axis=0)
        mine = jnp.where((z if axis == "y" else y) == 0, message(0), zero)
        for d in (2, 1, 3):
            if axis == "y":
                moves = [((i, j, 0), (i, j, d)) for i in range(4) for j in range(4)]
            else:
                moves = [((i, 0, j), (i, d, j)) for i in range(4) for j in range(4)]
            mine = mine + permute(message(d), moves)
        return mine

    mine_a = finish(hold_a, "y")
    mine_b = finish(hold_b, "z")

    inverse = lax.dynamic_index_in_dim(inverses, x, 0, keepdims=False)
    rounded = lax.reduce_precision(inverse, 8, 7)
    inverse = (rounded.astype(BF), (inverse - rounded).astype(BF))
    where = jnp.stack([core, x, y, z]).astype(jnp.int32)
    state = mine_a[:512].astype(F32) + mine_b[:512].astype(F32)
    state, *inverse = lax.optimization_barrier((state, *inverse))
    sent_0, = step(where, state, inverse)
    gots = [hop(sent_0, (0, 1)), hop(sent_0, (0, 3)), hop(sent_0, (0, 2))]

    piece_a, piece_b, _ = lax.optimization_barrier((mine_a[512:], mine_b[512:], sent_0))
    near_a, near_b = swap(piece_a, "y", 1), swap(piece_b, "z", 1)
    near_a, near_b, *gots = lax.optimization_barrier((near_a, near_b, *gots))

    def complete(piece, near, axis):
        two = jnp.stack([piece, near])
        return jnp.concatenate([two, swap(two, axis, 3)], axis=0).reshape(4, 3, 128, 128)

    top, bottom = complete(piece_a, near_a, "y"), complete(piece_b, near_b, "z")
    block = (top, bottom, lax.ppermute(top, "rhs", [(0, 1), (1, 0)]), lax.ppermute(bottom, "rhs", [(0, 1), (1, 0)]))

    panel_0 = jnp.where(x == 0, sent_0, gots[0] + gots[1] + gots[2])
    early_0 = lax.all_gather(panel_0, ("y", "z"), axis=0)
    state, sent_1 = step(where, state, inverse, block, 0, gots)
    gots_1 = [hop(sent_1, (1, 2)), hop(sent_1, (1, 3))]
    state, sent_2 = step(where, state, inverse, block, 1, gots_1)
    got = hop(sent_2, (2, 3))
    state, sent = step(where, state, inverse, block, 2, (got,))
    sent_2 = jnp.where(x == 2, sent_2, sent_1)
    sent = jnp.where(x == 3, sent, sent_2)
    far = hop(sent, (2, 0), (3, 1))
    back = hop(sent, (1, 0), (2, 1), (3, 2))
    wrap = hop(sent, (3, 0))
    panel_1 = jnp.where(x == 1, sent, jnp.where(x == 0, back, gots_1[0] + gots_1[1]))
    panel_2 = jnp.where(x == 2, sent, jnp.where(x == 3, got, jnp.where(x == 1, back, far)))
    panel_3 = jnp.where(x == 3, sent, jnp.where(x == 2, back, jnp.where(x == 1, far, wrap)))
    cat = lambda *v: jnp.concatenate(v, axis=0)
    parts = [panel_1[:384], cat(panel_1[384:], panel_2[:256]), cat(panel_2[256:], panel_3[:128]), panel_3[128:]]
    flat_factor = factor.reshape(2, 512, 1024)
    other_factor = lax.ppermute(flat_factor, "rhs", [(0, 1), (1, 0)])
    near, early_0, other_factor, far_late = spread(parts, early_0, other_factor)
    scalars = jnp.concatenate([places(y, z), jnp.stack([place, core])]).astype(jnp.int32)
    return update(scalars, flat_factor, other_factor, rhs, early_0, near, far_late)


def solution(mesh):
    grid = Mesh(mesh.devices.reshape(4, 4, 4, 2), ("y", "z", "x", "rhs"))
    return jax.shard_map(
        local,
        mesh=grid,
        in_specs=(P(None, ROWS, "rhs"), P(None, ROWS, None, "rhs"), P()),
        out_specs=P(None, ROWS, "rhs"),
        check_vma=False,
    )
```
